32 devices in a mesh: site: 8 (over z, y), mode: 4 (over x, core).
Axes of the slice: x: 2, y: 2, z: 4, core: 2. Of those that a mesh axis runs over, the one named last changes fastest.
Arguments:
- basis: bfloat16 [64, 400, 512], P('site', 'mode'), may hold values from -6 to 6
- images: bfloat16 [64, 400, 496], P('site', 'mode'), may hold values from -6 to 6
- hops: bfloat16 [64, 9, 400, 400], P('site', None, 'mode'), may hold values from -0.09375 to 0.09375
- neighbours: int32 [64, 8], P('site'), may hold values from 0 to 47, as said below
- rotation: bfloat16 [512, 512], replicated, may hold values from -0.25 to 0.25
Outputs:
- projected: float32 [512, 512], replicated
- rotated_basis: bfloat16 [64, 400, 512], P('site', 'mode')
- rotated_images: bfloat16 [64, 400, 512], P('site', 'mode')
The draws below stay inside these ranges and needn't reach their ends.
Inputs may be any that keep to these rules, and one draw needn't show every extreme that they name: `neighbours`: the blocks form a periodic 4 x 4 x 4 x 64/64 lattice. Group s = 8 t + 4 gx + 2 gy + gz holds the 2 x 2 x 2 cube of time slice t at spatial offsets 2 gx, 2 gy, 2 gz, stored in its own order. Columns 0, 1, 2 name the neighbour along x, y, z forward, columns 3, 4, 5 backward, column 6 the next time slice, column 7 the previous one, each as k * 8 + q with k and q as in the reference program.
All inputs are finite; a program needn't handle non-finite values.
Results may differ from the reference program's by a relative error of at most 0.0026.
Values may be sent and summed in bfloat16 or wider, within the bound.
No kernel may reach another device: no remote copies, remote signals or barrier semaphores. Data moves between devices by JAX's collectives and lax.ppermute only.
A program may use at most 64 MiB of HBM per device.

```python
import math
import jax
import jax.numpy as jnp

COARSE = 400
NVEC = 512
BLOCK = 16
HOPS = 9
NB_DEV = 8
OLD = 496
NBLK = 64
N_SITE = 8


def draw_neighbours(key, part):
    groups = NBLK // NB_DEV
    slices = groups // 8
    keys = jax.random.split(jax.random.fold_in(key, 17), groups)
    layout = jax.vmap(lambda k: jax.random.permutation(k, NB_DEV))(keys).astype(jnp.int32)
    inverse = jnp.argsort(layout, axis=1).astype(jnp.int32)
    group = jnp.arange(groups, dtype=jnp.int32)
    tslice = group // 8
    rest = group % 8
    ahead = (tslice + 1) % slices * 8 + rest
    behind = (tslice + slices - 1) % slices * 8 + rest
    forward_cols = []
    backward_cols = []
    for bit, piece in ((2, 1), (1, 2), (0, 3)):
        local_bit = jnp.bitwise_and(jnp.right_shift(layout, bit), 1)
        other = jnp.bitwise_xor(group, 1 << bit)
        flipped = jnp.bitwise_xor(layout, jnp.int32(1 << bit))
        pos_own = jnp.take_along_axis(inverse, flipped, axis=1)
        pos_other = inverse[other[:, None], flipped]
        fwd = jnp.where(local_bit == 0, pos_own, piece * NB_DEV + pos_other)
        bwd = jnp.where(local_bit == 1, pos_own, piece * NB_DEV + pos_other)
        forward_cols.append(fwd)
        backward_cols.append(bwd)
    next_col = 4 * NB_DEV + inverse[ahead[:, None], layout]
    prev_col = 5 * NB_DEV + inverse[behind[:, None], layout]
    table = jnp.stack(forward_cols + backward_cols + [next_col, prev_col], axis=2)
    return table.reshape(NBLK, 8).astype(jnp.int32)


def shard_levels(key, shape, cuts, least, top_value):
    def one(dim, parts):
        draws = jax.random.uniform(jax.random.fold_in(jax.random.fold_in(key, 6), dim), (parts,), jnp.float32, least / len(cuts), top_value / len(cuts))
        return jnp.repeat(jnp.exp(draws), shape[dim] // parts).reshape((-1,) + (1,) * (len(shape) - dim - 1))

    gain = one(*cuts[0])
    for cut in cuts[1:]:
        gain = gain * one(*cut)
    return gain


def gaussian(stream_key, shape, scale, limit, cuts=(), held_as=jnp.bfloat16):
    result = jax.random.normal(stream_key, shape, jnp.float32) * scale
    if len(cuts) > 0:
        result = shard_levels(stream_key, shape, cuts, -0.22, 0.18) * result
    return jnp.clip(result, min=-limit, max=limit).astype(held_as)


def setup_inputs(seed: int = 0) -> dict:
    streams_of = jax.random.split(jax.random.key(seed), 6)
    return {
        "basis": gaussian(streams_of[0], (NBLK, COARSE, NVEC), 1.0, 6.0, ((0, 8), (1, 4))),
        "images": gaussian(streams_of[1], (NBLK, COARSE, OLD), 1.0, 6.0, ((0, 8), (1, 4))),
        "hops": gaussian(streams_of[2], (NBLK, HOPS, COARSE, COARSE), (HOPS * COARSE) ** -0.5, 0.09375, ((0, 8), (2, 4))),
        "neighbours": draw_neighbours(jax.random.fold_in(streams_of[5], 71), 0),
        "rotation": gaussian(streams_of[4], (NVEC, NVEC), NVEC ** -0.5, 0.25),
    }


def neighbour_rows(neighbours):
    slices = N_SITE // 8
    block_rows = jnp.arange(NBLK, dtype=jnp.int32)
    group = block_rows // NB_DEV
    tslice = group // 8
    rest = group % 8
    ahead = (tslice + 1) % slices * 8 + rest
    behind = (tslice + slices - 1) % slices * 8 + rest
    candidates = jnp.stack([group, jnp.bitwise_xor(group, 4), jnp.bitwise_xor(group, 2), jnp.bitwise_xor(group, 1), ahead, behind], axis=1).astype(jnp.int32)
    columns = [block_rows]
    for direction in range(8):
        entry = neighbours[:, direction]
        source = jnp.take_along_axis(candidates, (entry // NB_DEV)[:, None].astype(jnp.int32), axis=1)[:, 0]
        columns.append((source * NB_DEV + entry % NB_DEV).astype(jnp.int32))
    return columns

def reference(basis, images, hops, neighbours, rotation):
    columns = neighbour_rows(neighbours)
    newest = basis[:, :, OLD:].astype(jnp.float32)
    total = jnp.zeros((NBLK, COARSE, BLOCK), jnp.float32)
    for direction in range(HOPS):
        matrices = hops[:, direction].astype(jnp.float32)
        total = total + jnp.einsum('boi,bik->bok', matrices, newest[columns[direction]])
    image_new = total.astype(jnp.bfloat16)
    images_all = jnp.concatenate([images, image_new], axis=2)
    flat_basis = basis.reshape(NBLK * COARSE, NVEC)
    flat_images = images_all.reshape(NBLK * COARSE, NVEC)
    norm_scale = 1.0 / math.sqrt(NBLK * COARSE)
    projected = jnp.dot(flat_basis.T, flat_images, preferred_element_type=jnp.float32) * norm_scale
    rotated_basis = jnp.dot(flat_basis, rotation, preferred_element_type=jnp.float32).astype(jnp.bfloat16)
    rotated_images = jnp.dot(flat_images, rotation, preferred_element_type=jnp.float32).astype(jnp.bfloat16)
    return (projected, rotated_basis.reshape(NBLK, COARSE, NVEC), rotated_images.reshape(NBLK, COARSE, NVEC))
```

```python
import functools
import math

import jax
import jax.numpy as jnp
from jax import lax
from jax.experimental import pallas as pl
from jax.experimental.pallas import tpu as pltpu
from jax.sharding import PartitionSpec as P

F32 = jnp.float32
BF16 = jnp.bfloat16
BOTH = ("site", "mode")
LANES = 128


def dot_nn(a, b):
    return lax.dot_general(a, b, (((1,), (0,)), ((), ())), preferred_element_type=F32)


def dot_tn(a, b):
    return lax.dot_general(a, b, (((0,), (0,)), ((), ())), preferred_element_type=F32)


def dot_nt(a, b):
    return lax.dot_general(a, b, (((1,), (1,)), ((), ())), preferred_element_type=F32)


def onehot(shape, test):
    rows = lax.broadcasted_iota(jnp.int32, shape, 0)
    cols = lax.broadcasted_iota(jnp.int32, shape, 1)
    return jnp.where(test(rows, cols), 1.0, 0.0).astype(BF16)


def split(x):
    high = x.astype(BF16)
    low = (x - high.astype(F32)).astype(BF16)
    return high, low


def place():
    mode = lax.axis_index("mode")
    site = lax.axis_index("site")
    core = lax.rem(mode, 2)
    half = lax.div(mode, 2)
    y = lax.rem(site, 2)
    z0 = lax.rem(lax.div(site, 2), 2)
    z1 = lax.rem(lax.div(site, 4), 2)
    return core, half, y, z0, z1


def pick(core, first, second):
    return first * (1 - core) + second * core


def rows_at(index, count):
    return pl.ds(pl.multiple_of(index * count, count), count)


def call(kernel, outs, *args, scratch=(), flops=10**8, moved=2 * 10**6):
    vmem = pl.BlockSpec(memory_space=pltpu.VMEM)
    return pl.pallas_call(
        kernel,
        out_shape=outs,
        in_specs=[vmem] * len(args),
        out_specs=jax.tree.map(lambda _: vmem, outs),
        scratch_shapes=scratch,
        compiler_params=pltpu.CompilerParams(vmem_limit_bytes=48 * 2**20),
        cost_estimate=pl.CostEstimate(flops=flops, bytes_accessed=moved, transcendentals=0),
    )(*args)


def shaped(rows, cols, dtype):
    return jax.ShapeDtypeStruct((rows, cols), dtype)


def first_kernel(nb, basis, images, pay):
    rows, nvec = basis.shape
    old = images.shape[1]
    blk = nvec - old
    core = place()[0]
    top = nvec // 2
    keep = basis[:, pl.ds(pl.multiple_of((1 - core) * top, top), top)]
    part = dot_tn(keep, images[...])
    high, low = split(part)
    pay[:top, :old] = high
    pay[:top, old:] = jnp.zeros((top, blk), BF16)
    pay[top : 2 * top, :old] = low
    pay[top : 2 * top, old:] = jnp.zeros((top, blk), BF16)
    wide = nb * blk
    last = basis[:, nvec - LANES :]
    spread = onehot((LANES, wide), lambda r, c: r - (LANES - blk) == lax.rem(c, blk))
    tiled = dot_nn(last, spread)
    row = lax.broadcasted_iota(jnp.int32, (rows, wide), 0)
    col = lax.broadcasted_iota(jnp.int32, (rows, wide), 1)
    tiled = jnp.where(lax.rem(row, nb) == lax.div(col, blk), tiled, 0.0).astype(BF16)
    gather = onehot((rows, LANES), lambda r, c: lax.div(r, nb) == c)
    flipped = dot_tn(tiled, gather).astype(BF16)
    groups = nvec // LANES
    each = wide // groups
    for g in range(groups):
        pay[2 * top :, g * LANES : (g + 1) * LANES] = flipped[g * each : (g + 1) * each]


def keep_kernel(basis, images, kept):
    nvec = basis.shape[1]
    old = images.shape[1]
    core = place()[0]
    top = nvec // 2
    mine = basis[:, pl.ds(pl.multiple_of(core * top, top), top)]
    kept[:, :old] = dot_tn(mine, images[...])
    kept[:, old:] = jnp.zeros((top, nvec - old), F32)


def rotate_kernel(basis, rotation, out):
    out[...] = dot_nn(basis[...], rotation[...]).astype(BF16)


def joined(kept, got, start, count):
    whole = kept.shape[0]
    rows = pl.ds(pl.multiple_of(start, count), count)
    lows = pl.ds(pl.multiple_of(start + whole, count), count)
    return kept[rows, :] + (got[rows, :].astype(F32) + got[lows, :].astype(F32))


def second_kernel(kept, got, pay, out, rest):
    core, half, y, z0, z1 = place()
    whole = kept.shape[0]
    n = whole // 2
    bit = pick(core, half, y)
    out[:n, :], out[n : 2 * n, :] = split(joined(kept, got, (1 - bit) * n, n))
    rest[...] = joined(kept, got, bit * n, n)
    each = got.shape[0] - 2 * whole
    out[pl.ds(pl.multiple_of(2 * n + core * each, each), each), :] = pay[2 * whole :, :]
    out[pl.ds(pl.multiple_of(2 * n + (1 - core) * each, each), each), :] = got[2 * whole :, :]


def third_kernel(kept, got, pay, out, rest):
    core, half, y, z0, z1 = place()
    whole = kept.shape[0]
    n = whole // 2
    bit = pick(core, y, half)
    out[:n, :], out[n : 2 * n, :] = split(joined(kept, got, (1 - bit) * n, n))
    rest[...] = joined(kept, got, bit * n, n)
    each = got.shape[0] - 2 * whole
    at = pick(core, half, 0)
    out[pl.ds(pl.multiple_of(2 * n + at * each, each), each), :] = pay[2 * whole :, :]
    out[pl.ds(pl.multiple_of(2 * n + (1 - at) * each, each), each), :] = got[2 * whole :, :]


def fourth_kernel(kept, got, pay, out, rest, side, hold):
    core, half, y, z0, z1 = place()
    whole = kept.shape[0]
    n = whole // 2
    bit = pick(core, z0, z1)
    out[:n, :], out[n : 2 * n, :] = split(joined(kept, got, (1 - bit) * n, n))
    rest[...] = joined(kept, got, bit * n, n)
    area = got.shape[0] - 2 * whole
    each = area // 2
    hold[:area, :] = pay[2 * whole :, :]
    hold[area:, :] = got[2 * whole :, :]
    for j in range(2):
        other = j * (1 - half) + (1 - j) * half
        own = pick(core, j, 2 * other)
        near = pick(core, 2 + j, 1 + 2 * other)
        out[2 * n + j * each : 2 * n + (j + 1) * each, :] = hold[rows_at(own, each), :]
        side[j * each : (j + 1) * each, :] = hold[rows_at(near, each), :]


def fifth_kernel(kept, got, out):
    n = kept.shape[0]
    total = kept[...] + (got[:n, :].astype(F32) + got[n : 2 * n, :].astype(F32))
    out[:n, :], out[n:, :] = split(total)


def assemble(area, spots, coarse):
    rows, nvec = area.shape
    groups = nvec // LANES
    modes = spots
    each = rows // modes
    share = coarse // modes
    lines = []
    for g in range(groups):
        lines.append(
            jnp.concatenate(
                [area[m * each : (m + 1) * each, g * LANES : (g + 1) * LANES] for m in range(modes)],
                axis=1,
            )
        )
    flat = jnp.concatenate(lines, axis=0)
    shift = onehot(
        (modes * LANES, coarse),
        lambda r, c: (lax.rem(r, LANES) < share) & (lax.div(r, LANES) * share + lax.rem(r, LANES) == c),
    )
    return dot_nn(flat, shift).astype(BF16)


def weights(table, step_hop, store, mixed, nb, blk):
    for b in range(nb):
        entry = table[b, step_hop]
        mixed[b * blk : (b + 1) * blk, :] = store[pl.ds(pl.multiple_of(entry * blk, blk), blk), :]


def stencil_near(order, table, nb, blk, spots, own_ref, side_ref, hops, total, own_out, store, mixed):
    step = pl.program_id(0)
    coarse = store.shape[1]
    wide = nb * blk

    @pl.when(step == 0)
    def _():
        own = assemble(own_ref[...], spots, coarse)
        own_out[...] = own
        near = assemble(side_ref[...], spots, coarse)
        for k in (0, 1, 2, 4, 5):
            store[k * wide : (k + 1) * wide, :] = own
        store[3 * wide : 4 * wide, :] = near

    weights(table, order[step], store, mixed, nb, blk)
    part = dot_nt(hops[...], mixed[...])

    @pl.when(step == 0)
    def _():
        total[...] = part

    @pl.when(step > 0)
    def _():
        total[...] += part


def run_near(order, table, own, side, hops, nb, blk, spots):
    count, rows, coarse = hops.shape
    wide = nb * blk
    steps = len(order)

    def kernel(order_ref, table_ref, own_ref, side_ref, hops_ref, total, own_out, store, mixed):
        stencil_near(
            order_ref, table_ref, nb, blk, spots, own_ref, side_ref, hops_ref, total, own_out, store, mixed
        )

    spec = pltpu.PrefetchScalarGridSpec(
        num_scalar_prefetch=2,
        grid=(steps,),
        in_specs=[
            pl.BlockSpec(own.shape, lambda i, o, t: (0, 0)),
            pl.BlockSpec(side.shape, lambda i, o, t: (0, 0)),
            pl.BlockSpec((None, rows, coarse), lambda i, o, t: (o[i], 0, 0)),
        ],
        out_specs=[
            pl.BlockSpec((rows, wide), lambda i, o, t: (0, 0)),
            pl.BlockSpec((wide, coarse), lambda i, o, t: (0, 0)),
        ],
        scratch_shapes=[pltpu.VMEM((6 * wide, coarse), BF16), pltpu.VMEM((wide, coarse), BF16)],
    )
    return pl.pallas_call(
        kernel,
        grid_spec=spec,
        out_shape=[shaped(rows, wide, F32), shaped(wide, coarse, BF16)],
        compiler_params=pltpu.CompilerParams(vmem_limit_bytes=32 * 2**20),
        cost_estimate=pl.CostEstimate(
            flops=2 * steps * rows * coarse * wide, bytes_accessed=2 * steps * rows * coarse, transcendentals=0
        ),
    )(jnp.array(order, jnp.int32), table, own, side, hops)


def run_far(order, table, own, mine, other, times, total, basis, old, hops, nb, blk, spots):
    count, rows, coarse = hops.shape
    wide = nb * blk
    steps = len(order)
    nvec = basis.shape[1]
    nold = old.shape[0]
    n_times = len(times)

    def kernel(order_ref, table_ref, own_ref, mine_ref, other_ref, *refs):
        time_refs = refs[:n_times]
        total_ref, basis_ref, old_ref, hops_ref, masked, pay, store, mixed, acc = refs[n_times:]
        step = pl.program_id(0)
        core = place()[0]

        @pl.when(step == 0)
        def _():
            own = own_ref[...]
            for k in (0, 3, 4, 5):
                store[k * wide : (k + 1) * wide, :] = own
            first = assemble(mine_ref[...], spots, coarse)
            second = assemble(other_ref[...], spots, coarse)
            store[rows_at(2 - core, wide), :] = first
            store[rows_at(1 + core, wide), :] = second
            for k, ref in enumerate(time_refs):
                store[(4 + k) * wide : (5 + k) * wide, :] = assemble(ref[...], spots, coarse)

        weights(table_ref, order_ref[step], store, mixed, nb, blk)
        part = dot_nt(hops_ref[...], mixed[...])

        @pl.when(step == 0)
        def _():
            acc[...] = total_ref[...] + part

        @pl.when(step > 0)
        def _():
            acc[...] += part

        @pl.when(step == steps - 1)
        def _():
            row = lax.broadcasted_iota(jnp.int32, (rows, wide), 0)
            col = lax.broadcasted_iota(jnp.int32, (rows, wide), 1)
            chosen = jnp.where(lax.rem(row, nb) == lax.div(col, blk), acc[...], 0.0).astype(BF16)
            masked[...] = chosen
            fold = onehot((blk, wide), lambda r, c: lax.rem(c, blk) == r)
            flat = dot_nt(fold, chosen).astype(BF16)
            new = dot_nn(flat, basis_ref[...])
            pay[:nold, :] = old_ref[...]
            pay[nold : nold + blk, :], pay[nold + blk :, :] = split(new)

    spec = pltpu.PrefetchScalarGridSpec(
        num_scalar_prefetch=2,
        grid=(steps,),
        in_specs=[pl.BlockSpec(a.shape, lambda i, o, t: (0, 0)) for a in (own, mine, other, *times, total, basis, old)]
        + [pl.BlockSpec((None, rows, coarse), lambda i, o, t: (o[i], 0, 0))],
        out_specs=[
            pl.BlockSpec((rows, wide), lambda i, o, t: (0, 0)),
            pl.BlockSpec((nold + 2 * blk, nvec), lambda i, o, t: (0, 0)),
        ],
        scratch_shapes=[
            pltpu.VMEM((6 * wide, coarse), BF16),
            pltpu.VMEM((wide, coarse), BF16),
            pltpu.VMEM((rows, wide), F32),
        ],
    )
    return pl.pallas_call(
        kernel,
        grid_spec=spec,
        out_shape=[shaped(rows, wide, BF16), shaped(nold + 2 * blk, nvec, BF16)],
        compiler_params=pltpu.CompilerParams(vmem_limit_bytes=32 * 2**20),
        cost_estimate=pl.CostEstimate(
            flops=2 * steps * rows * coarse * wide, bytes_accessed=2 * steps * rows * coarse, transcendentals=0
        ),
    )(jnp.array(order, jnp.int32), table, own, mine, other, *times, total, basis, old, hops)


def turn_kernel(nb, images, masked, rotation, out):
    old = images.shape[1]
    tail = rotation[old:, :]
    deep = jnp.concatenate([tail] * nb, axis=0)
    out[...] = (dot_nn(images[...], rotation[:old, :]) + dot_nn(masked[...], deep)).astype(BF16)


def value(ref, start, count):
    return ref[start : start + count, :].astype(F32) + ref[start + count : start + 2 * count, :].astype(F32)


def extra_kernel(n, blk, pay, got, out):
    out[:n, :], out[n : 2 * n, :] = split(value(pay, 0, n) + value(got, 0, n))
    out[2 * n : 2 * n + blk, :], out[2 * n + blk :, :] = split(value(pay, 2 * n, blk) + value(got, 2 * n, blk))


def settle_kernel(n, blk, scale, pay, got, out):
    out[:n, :] = ((value(pay, 0, n) + value(got, 0, n)) * scale).astype(BF16)
    out[n : n + blk, :], out[n + blk :, :] = split(value(pay, 2 * n, blk) + value(got, 2 * n, blk))


def grow_kernel(n, blk, chooser, pay, got, out):
    bit = chooser(*place())
    out[rows_at(bit, n), :] = pay[:n, :]
    out[rows_at(1 - bit, n), :] = got[:n, :]
    out[2 * n : 2 * n + blk, :], out[2 * n + blk :, :] = split(value(pay, n, blk) + value(got, n, blk))


def final_kernel(n, blk, scale, pay, got, out):
    nvec = out.shape[1]
    core = place()[0]
    out[rows_at(core, n), :] = pay[:n, :].astype(F32)
    out[rows_at(1 - core, n), :] = got[:n, :].astype(F32)
    new = (value(pay, n, blk) + value(got, n, blk)) * scale
    tall = jnp.concatenate([jnp.zeros((LANES - blk, nvec), F32), new], axis=0)
    flipped = tall.T
    lane = lax.broadcasted_iota(jnp.int32, (nvec, LANES), 1)
    out[:, nvec - LANES :] = jnp.where(lane < LANES - blk, out[:, nvec - LANES :], flipped)


def local(basis, images, hops, neighbours, rotation):
    nb, modes_here, nvec = basis.shape
    old = images.shape[2]
    blk = nvec - old
    sites = lax.axis_size("site")
    spots = lax.axis_size("mode")
    count = sites * spots
    rows = nb * modes_here
    coarse = hops.shape[3]
    wide = nb * blk
    chunk = wide * LANES // nvec
    scale = 1.0 / math.sqrt(count * rows)

    def send(x, first, second):
        pairs = [(d, d ^ (second if d % 2 else first)) for d in range(count)]
        return lax.ppermute(x, BOTH, pairs)

    core_hop, x_hop, y_hop, z0_hop, z1_hop = 1, 2, spots, 2 * spots, 4 * spots

    flat_basis = jnp.transpose(basis, (1, 0, 2)).reshape(rows, nvec)
    flat_images = jnp.transpose(images, (1, 0, 2)).reshape(rows, old)
    flat_hops = jnp.transpose(hops, (1, 2, 0, 3)).reshape(hops.shape[1], rows, coarse)
    own_rows = jnp.arange(nb, dtype=jnp.int32)
    table = jnp.concatenate([own_rows[:, None], neighbours], axis=1)

    half = nvec // 2
    pay0 = call(functools.partial(first_kernel, nb), shaped(nvec + chunk, nvec, BF16), flat_basis, flat_images)
    got0 = send(pay0, core_hop, core_hop)
    kept0 = call(keep_kernel, shaped(half, nvec, F32), flat_basis, flat_images)
    pay1, kept1 = call(
        second_kernel,
        (shaped(half + 2 * chunk, nvec, BF16), shaped(half // 2, nvec, F32)),
        kept0,
        got0,
        pay0,
    )
    got1 = send(pay1, x_hop, y_hop)
    turned_basis = call(rotate_kernel, shaped(rows, nvec, BF16), flat_basis, rotation)
    pay2, kept2 = call(
        third_kernel,
        (shaped(half // 2 + 4 * chunk, nvec, BF16), shaped(half // 4, nvec, F32)),
        kept1,
        got1,
        pay1,
    )
    got2 = send(pay2, y_hop, x_hop)
    pay3, kept3, side = call(
        fourth_kernel,
        (shaped(half // 4 + 4 * chunk, nvec, BF16), shaped(half // 8, nvec, F32), shaped(4 * chunk, nvec, BF16)),
        kept2,
        got2,
        pay2,
        scratch=[pltpu.VMEM((8 * chunk, nvec), BF16)],
    )
    n = half // 8
    got3 = send(pay3, z0_hop, z1_hop)
    own = pay3[2 * n :, :]
    times = []
    near_order = [0, 3, 6]
    far_order = [1, 4, 2, 5]
    if sites > 8:
        step = 8 * spots
        times = [
            lax.ppermute(own, BOTH, [((d + sign * step) % count, d) for d in range(count)]) for sign in (1, -1)
        ]
        far_order = far_order + [7, 8]
    else:
        near_order = near_order + [7, 8]
    total, own_flat = run_near(near_order, table, own, side, flat_hops, nb, blk, spots)
    mine = got3[2 * n :, :]
    other = send(mine, core_hop, core_hop)
    old_pay = call(fifth_kernel, shaped(2 * n, nvec, BF16), kept3, got3)
    masked, payc = run_far(
        far_order, table, own_flat, mine, other, times, total, flat_basis, old_pay, flat_hops, nb, blk, spots
    )
    gotc = send(payc, z1_hop, z0_hop)
    turned_images = call(functools.partial(turn_kernel, nb), shaped(rows, nvec, BF16), flat_images, masked, rotation)
    hop = 8 * spots
    while hop < count:
        payc = call(functools.partial(extra_kernel, n, blk), shaped(2 * n + 2 * blk, nvec, BF16), payc, gotc)
        gotc = send(payc, hop, hop)
        hop *= 2
    payc = call(functools.partial(settle_kernel, n, blk, scale), shaped(n + 2 * blk, nvec, BF16), payc, gotc)
    gotc = send(payc, z0_hop, z1_hop)
    payc = call(
        functools.partial(grow_kernel, n, blk, lambda core, half, y, z0, z1: pick(core, z0, z1)),
        shaped(2 * n + 2 * blk, nvec, BF16),
        payc,
        gotc,
    )
    gotc = send(payc, y_hop, x_hop)
    payc = call(
        functools.partial(grow_kernel, 2 * n, blk, lambda core, half, y, z0, z1: pick(core, y, half)),
        shaped(4 * n + 2 * blk, nvec, BF16),
        payc,
        gotc,
    )
    gotc = send(payc, x_hop, y_hop)
    payc = call(
        functools.partial(grow_kernel, 4 * n, blk, lambda core, half, y, z0, z1: pick(core, half, y)),
        shaped(8 * n + 2 * blk, nvec, BF16),
        payc,
        gotc,
    )
    gotc = send(payc, core_hop, core_hop)
    projected = call(functools.partial(final_kernel, 8 * n, blk, scale), shaped(nvec, nvec, F32), payc, gotc)

    def back(x):
        return jnp.transpose(x.reshape(modes_here, nb, nvec), (1, 0, 2))

    return projected, back(turned_basis), back(turned_images)


def solution(mesh):
    placed = (
        P("site", "mode", None),
        P("site", "mode", None),
        P("site", None, "mode", None),
        P("site", None),
        P(),
    )
    return jax.shard_map(
        local,
        mesh=mesh,
        in_specs=placed,
        out_specs=(P(), P("site", "mode", None), P("site", "mode", None)),
        check_vma=False,
    )
```

```python
import functools
import math

import jax
import jax.numpy as jnp
from jax import lax
from jax.experimental import pallas as pl
from jax.experimental.pallas import tpu as pltpu
from jax.sharding import PartitionSpec as P


F32 = jnp.float32
BF16 = jnp.bfloat16
BOTH = ("site", "mode")
LANES = 128


def dot_nn(a, b):
    return lax.dot_general(a, b, (((1,), (0,)), ((), ())), preferred_element_type=F32)


def dot_tn(a, b):
    return lax.dot_general(a, b, (((0,), (0,)), ((), ())), preferred_element_type=F32)


def onehot(shape, test):
    rows = lax.broadcasted_iota(jnp.int32, shape, 0)
    cols = lax.broadcasted_iota(jnp.int32, shape, 1)
    return jnp.where(test(rows, cols), 1.0, 0.0).astype(BF16)


def split(x):
    high = x.astype(BF16)
    low = (x - high.astype(F32)).astype(BF16)
    return high, low


def place():
    mode = lax.axis_index("mode")
    site = lax.axis_index("site")
    core = lax.rem(mode, 2)
    half = lax.div(mode, 2)
    y = lax.rem(site, 2)
    z0 = lax.rem(lax.div(site, 2), 2)
    z1 = lax.rem(lax.div(site, 4), 2)
    return core, half, y, z0, z1


def pick(core, first, second):
    return first * (1 - core) + second * core


def rows_at(index, count):
    return pl.ds(pl.multiple_of(index * count, count), count)


def call(kernel, outs, *args, scratch=(), flops=10**8, moved=2 * 10**6, smem=()):
    vmem = pl.BlockSpec(memory_space=pltpu.VMEM)
    scalars = pl.BlockSpec(memory_space=pltpu.SMEM)
    return pl.pallas_call(
        kernel,
        out_shape=outs,
        in_specs=[scalars if i in smem else vmem for i in range(len(args))],
        out_specs=jax.tree.map(lambda _: vmem, outs),
        scratch_shapes=scratch,
        compiler_params=pltpu.CompilerParams(vmem_limit_bytes=16 * 2**20),
        cost_estimate=pl.CostEstimate(flops=flops, bytes_accessed=moved, transcendentals=0),
    )(*args)


def shaped(rows, cols, dtype):
    return jax.ShapeDtypeStruct((rows, cols), dtype)


def first_kernel(nb, basis, images, pay):
    rows, nvec = basis.shape
    old = images.shape[1]
    blk = nvec - old
    core = place()[0]
    top = nvec // 2
    keep = basis[:, pl.ds(pl.multiple_of((1 - core) * top, top), top)]
    part = dot_tn(keep, images[...])
    high, low = split(part)
    pay[:top, :old] = high
    pay[:top, old:] = jnp.zeros((top, blk), BF16)
    pay[top : 2 * top, :old] = low
    pay[top : 2 * top, old:] = jnp.zeros((top, blk), BF16)
    wide = nb * blk
    last = basis[:, nvec - LANES :]
    spread = onehot((LANES, wide), lambda r, c: r - (LANES - blk) == lax.rem(c, blk))
    tiled = dot_nn(last, spread)
    row = lax.broadcasted_iota(jnp.int32, (rows, wide), 0)
    col = lax.broadcasted_iota(jnp.int32, (rows, wide), 1)
    tiled = jnp.where(lax.rem(row, nb) == lax.div(col, blk), tiled, 0.0).astype(BF16)
    gather = onehot((LANES, rows), lambda r, c: lax.div(c, nb) == r)
    merged = dot_nn(gather, tiled).astype(BF16)
    groups = nvec // LANES
    each = LANES // groups
    for g in range(groups):
        pay[2 * top :, g * LANES : (g + 1) * LANES] = merged[g * each : (g + 1) * each]


def keep_kernel(basis, images, kept):
    nvec = basis.shape[1]
    old = images.shape[1]
    core = place()[0]
    top = nvec // 2
    mine = basis[:, pl.ds(pl.multiple_of(core * top, top), top)]
    kept[:, :old] = dot_tn(mine, images[...])
    kept[:, old:] = jnp.zeros((top, nvec - old), F32)


def rotate_kernel(basis, rotation, out):
    out[...] = dot_nn(basis[...], rotation[...]).astype(BF16)


def joined(kept, got, start, count):
    whole = kept.shape[0]
    rows = pl.ds(pl.multiple_of(start, count), count)
    lows = pl.ds(pl.multiple_of(start + whole, count), count)
    return kept[rows, :] + (got[rows, :].astype(F32) + got[lows, :].astype(F32))


def second_kernel(kept, got, pay, out, rest, pair):
    core, half, y, _, _ = place()
    whole = kept.shape[0]
    n = whole // 2
    bit = pick(core, half, y)
    out[:n, :], out[n : 2 * n, :] = split(joined(kept, got, (1 - bit) * n, n))
    rest[...] = joined(kept, got, bit * n, n)
    each = got.shape[0] - 2 * whole
    pair[rows_at(core, each), :] = pay[2 * whole :, :]
    pair[rows_at(1 - core, each), :] = got[2 * whole :, :]
    out[2 * n :, :] = pair[...]


def third_kernel(kept, got, pair, far, out, rest):
    core, half, _, z0, _ = place()
    whole = kept.shape[0]
    n = whole // 2
    bit = pick(core, z0, half)
    out[:n, :], out[n : 2 * n, :] = split(joined(kept, got, (1 - bit) * n, n))
    rest[...] = joined(kept, got, bit * n, n)
    each = pair.shape[0]
    at = pick(core, 1 - half, 0)
    out[pl.ds(pl.multiple_of(2 * n + at * each, each), each), :] = got[2 * whole :, :]
    out[pl.ds(pl.multiple_of(2 * n + (1 - at) * each, each), each), :] = jnp.where(
        core == 0, pair[...], far[...]
    )


def fourth_kernel(kept, got, far, out, rest, cross):
    core, _, _, z0, z1 = place()
    whole = kept.shape[0]
    n = whole // 2
    bit = pick(core, z1, z0)
    out[:n, :], out[n:, :] = split(joined(kept, got, (1 - bit) * n, n))
    rest[...] = joined(kept, got, bit * n, n)
    area = got.shape[0] - 2 * whole
    cross[:area, :] = got[2 * whole :, :]
    cross[area:, :] = far[...]


def setup_kernel(near, nb, blk, spots, table, perms, shift):
    hops = perms.shape[0]
    wide = nb * blk
    coarse = shift.shape[0]
    share = coarse // spots
    row = lax.broadcasted_iota(jnp.int32, (2 * wide, wide), 0)
    col = lax.broadcasted_iota(jnp.int32, (2 * wide, wide), 1)
    for hop in range(hops):
        wanted = lax.rem(col, blk)
        for b in range(nb):
            entry = table[b, hop]
            q = lax.rem(entry, nb)
            base = q * blk
            if hop not in near:
                base = base + jnp.where(entry >= nb, wide, 0)
            wanted = wanted + jnp.where(lax.div(col, blk) == b, base, 0)
        perms[hop] = jnp.where(row == wanted, 1.0, 0.0).astype(BF16)
    shift[...] = onehot(
        (coarse, spots * LANES),
        lambda r, c: (lax.rem(c, LANES) < share) & (lax.div(c, LANES) * share + lax.rem(c, LANES) == r),
    )


def stack(ref, at, piece):
    rows, nvec = piece.shape
    groups = nvec // LANES
    each = LANES // groups
    chunks = rows // each
    parts = [
        piece[m * each : (m + 1) * each, g * LANES : (g + 1) * LANES] for m in range(chunks) for g in range(groups)
    ]
    ref[rows_at(at, chunks * LANES), :] = jnp.concatenate(parts, axis=0)


def near_kernel(order, pair, got, crossed, hops, perms, shift, total, own_out, column):
    core, half, _, _, _ = place()
    each = pair.shape[0]
    wide = own_out.shape[1]
    area = got.shape[0]
    stack(column, half, pair[...])
    stack(column, 1 - half, jnp.where(core == 0, got[area - each :, :], crossed[...]))
    own = dot_nn(shift[...], column[...]).astype(BF16)
    own_out[...] = own
    rows = total.shape[0]
    mixed = [dot_nn(own, perms[hop, :wide, :]).astype(BF16) for hop in order]
    step = rows // 2
    for r in range(2):
        span = pl.ds(r * step, step)
        part = dot_nn(hops[order[0], span, :], mixed[0])
        for i in range(1, len(order)):
            part = part + dot_nn(hops[order[i], span, :], mixed[i])
        total[span, :] = part


def far_kernel(nb, blk, own, got2, cross, far, got1, crossed, total, basis, hops, perms, shift, *refs):
    times, (masked, new_out, column) = refs[:-3], refs[-3:]
    core, half, _, _, _ = place()
    each = far.shape[0]
    wide = own.shape[1]
    rows = basis.shape[0]
    nvec = basis.shape[1]
    first = core == 0
    mine = got2[got2.shape[0] - 2 * each :, :]
    theirs = cross[: 2 * each, :]
    sites = []
    one = jnp.where(first, theirs, mine)
    two = jnp.where(first, mine, theirs)
    stack(column.at[0], half, jnp.where(first, crossed[...], got1[got1.shape[0] - each :, :]))
    stack(column.at[0], 1 - half, one[:each])
    stack(column.at[1], half, jnp.where(first, cross[2 * each :, :], far[...]))
    stack(column.at[1], 1 - half, one[each:])
    stack(column.at[2], 0, two)
    near_site = dot_nn(shift[...], column[0]).astype(BF16)
    long_site = dot_nn(shift[...], column[1]).astype(BF16)
    mid_site = dot_nn(shift[...], column[2]).astype(BF16)
    sites = {1: long_site, 4: long_site, 2: mid_site, 5: mid_site, 3: near_site, 6: near_site}
    for k, ref in enumerate(times):
        sites[7 + k] = ref[...]
    order = sorted(sites)
    mixed = [
        (dot_nn(own[...], perms[hop, :wide, :]) + dot_nn(sites[hop], perms[hop, wide:, :])).astype(BF16)
        for hop in order
    ]
    step = rows // 2
    sums = jnp.zeros((wide, nvec), F32)
    for r in range(2):
        span = pl.ds(r * step, step)
        part = total[span, :]
        for i, hop in enumerate(order):
            part = part + dot_nn(hops[hop, span, :], mixed[i])
        row = lax.broadcasted_iota(jnp.int32, (step, wide), 0)
        col = lax.broadcasted_iota(jnp.int32, (step, wide), 1)
        chosen = jnp.where(lax.rem(row, nb) == lax.div(col, blk), part, 0.0).astype(BF16)
        masked[span, :] = chosen
        sums = sums + dot_tn(chosen, basis[span, :])
    new = sums[:blk]
    for b in range(1, nb):
        new = new + sums[b * blk : (b + 1) * blk]
    new_out[:blk, :], new_out[blk:, :] = split(new)


def join_kernel(kept, got, new, out):
    n = kept.shape[0]
    total = kept[...] + (got[:n, :].astype(F32) + got[n:, :].astype(F32))
    out[:n, :], out[n : 2 * n, :] = split(total)
    out[2 * n :, :] = new[...]


def turn_kernel(nb, images, masked, rotation, out):
    old = images.shape[1]
    tail = rotation[old:, :]
    deep = jnp.concatenate([tail] * nb, axis=0)
    out[...] = (dot_nn(images[...], rotation[:old, :]) + dot_nn(masked[...], deep)).astype(BF16)


def value(ref, start, count):
    return ref[start : start + count, :].astype(F32) + ref[start + count : start + 2 * count, :].astype(F32)


def extra_kernel(n, blk, pay, got, out):
    out[:n, :], out[n : 2 * n, :] = split(value(pay, 0, n) + value(got, 0, n))
    out[2 * n : 2 * n + blk, :], out[2 * n + blk :, :] = split(value(pay, 2 * n, blk) + value(got, 2 * n, blk))


def settle_kernel(n, blk, scale, pay, got, out):
    out[:n, :] = ((value(pay, 0, n) + value(got, 0, n)) * scale).astype(BF16)
    out[n : n + blk, :], out[n + blk :, :] = split(value(pay, 2 * n, blk) + value(got, 2 * n, blk))


def grow_kernel(n, blk, chooser, pay, got, out):
    bit = chooser(*place())
    out[rows_at(bit, n), :] = pay[:n, :]
    out[rows_at(1 - bit, n), :] = got[:n, :]
    out[2 * n : 2 * n + blk, :], out[2 * n + blk :, :] = split(value(pay, n, blk) + value(got, n, blk))


def final_kernel(n, blk, scale, pay, got, out):
    nvec = out.shape[1]
    core = place()[0]
    out[rows_at(core, n), :] = pay[:n, :].astype(F32)
    out[rows_at(1 - core, n), :] = got[:n, :].astype(F32)
    new = (value(pay, n, blk) + value(got, n, blk)) * scale
    tall = jnp.concatenate([jnp.zeros((LANES - blk, nvec), F32), new], axis=0)
    flipped = tall.T
    lane = lax.broadcasted_iota(jnp.int32, (nvec, LANES), 1)
    out[:, nvec - LANES :] = jnp.where(lane < LANES - blk, out[:, nvec - LANES :], flipped)


def program(basis, images, hops, neighbours, rotation):
    nb, modes_here, nvec = basis.shape
    old = images.shape[2]
    blk = nvec - old
    sites = lax.axis_size("site")
    spots = lax.axis_size("mode")
    count = sites * spots
    rows = nb * modes_here
    coarse = hops.shape[3]
    wide = nb * blk
    chunk = wide * LANES // nvec
    scale = 1.0 / math.sqrt(count * rows)

    def send(x, first, second):
        pairs = [(d, d ^ hop) for d in range(count) for hop in [second if d % 2 else first] if hop]
        return lax.ppermute(x, BOTH, pairs)

    core_hop, x_hop, y_hop, z0_hop, z1_hop = 1, 2, spots, 2 * spots, 4 * spots

    flat_basis = jnp.transpose(basis, (1, 0, 2)).reshape(rows, nvec)
    flat_images = jnp.transpose(images, (1, 0, 2)).reshape(rows, old)
    flat_hops = jnp.transpose(hops, (1, 2, 0, 3)).reshape(hops.shape[1], rows, coarse)
    own_rows = jnp.arange(nb, dtype=jnp.int32)
    table = jnp.concatenate([own_rows[:, None], neighbours], axis=1)
    near_order = [0] if sites > 8 else [0, 7, 8]

    half = nvec // 2
    n = half // 8
    pay0 = call(functools.partial(first_kernel, nb), shaped(nvec + chunk, nvec, BF16), flat_basis, flat_images)
    got0 = send(pay0, core_hop, core_hop)
    kept0 = call(keep_kernel, shaped(half, nvec, F32), flat_basis, flat_images)
    pay1, kept1, pair = call(
        second_kernel,
        (shaped(half + 2 * chunk, nvec, BF16), shaped(half // 2, nvec, F32), shaped(2 * chunk, nvec, BF16)),
        kept0,
        got0,
        pay0,
    )
    got1 = send(pay1, x_hop, y_hop)
    far = send(pair, 0, z1_hop)
    perms, shift = call(
        functools.partial(setup_kernel, near_order, nb, blk, spots),
        (
            jax.ShapeDtypeStruct((hops.shape[1], 2 * wide, wide), BF16),
            shaped(coarse, spots * LANES, BF16),
        ),
        table,
        smem=(0,),
    )
    turned_basis = call(rotate_kernel, shaped(rows, nvec, BF16), flat_basis, rotation)
    pay2, kept2 = call(
        third_kernel,
        (shaped(half // 2 + 4 * chunk, nvec, BF16), shaped(half // 4, nvec, F32)),
        kept1,
        got1,
        pair,
        far,
    )
    got2 = send(pay2, z0_hop, x_hop)
    crossed = send(got1[half:, :], core_hop, core_hop)
    total, own = call(
        functools.partial(near_kernel, near_order),
        (shaped(rows, wide, F32), shaped(coarse, wide, BF16)),
        pair,
        got1,
        crossed,
        flat_hops,
        perms,
        shift,
        scratch=[pltpu.VMEM((spots * LANES, wide), BF16)],
    )
    times = []
    if sites > 8:
        gap = 8 * spots
        times = [lax.ppermute(own, BOTH, [((d + sign * gap) % count, d) for d in range(count)]) for sign in (1, -1)]
    pay3, kept3, cross_pay = call(
        fourth_kernel,
        (shaped(half // 4, nvec, BF16), shaped(half // 8, nvec, F32), shaped(6 * chunk, nvec, BF16)),
        kept2,
        got2,
        far,
    )
    cross = send(cross_pay, core_hop, core_hop)
    got3 = send(pay3, z1_hop, z0_hop)
    masked, new = call(
        functools.partial(far_kernel, nb, blk),
        (shaped(rows, wide, BF16), shaped(2 * blk, nvec, BF16)),
        own,
        got2,
        cross,
        far,
        got1,
        crossed,
        total,
        flat_basis,
        flat_hops,
        perms,
        shift,
        *times,
        scratch=[pltpu.VMEM((3, spots * LANES, wide), BF16)],
    )
    payc = call(join_kernel, shaped(2 * n + 2 * blk, nvec, BF16), kept3, got3, new)
    gotc = send(payc, y_hop, z1_hop)
    turned_images = call(functools.partial(turn_kernel, nb), shaped(rows, nvec, BF16), flat_images, masked, rotation)
    hop = 8 * spots
    while hop < count:
        payc = call(functools.partial(extra_kernel, n, blk), shaped(2 * n + 2 * blk, nvec, BF16), payc, gotc)
        gotc = send(payc, hop, hop)
        hop *= 2
    payc = call(functools.partial(settle_kernel, n, blk, scale), shaped(n + 2 * blk, nvec, BF16), payc, gotc)
    steps = (
        (z1_hop, z0_hop, lambda core, half, y, z0, z1: pick(core, z1, z0)),
        (z0_hop, x_hop, lambda core, half, y, z0, z1: pick(core, z0, half)),
        (x_hop, y_hop, lambda core, half, y, z0, z1: pick(core, half, y)),
    )
    for first, second, chooser in steps:
        gotc = send(payc, first, second)
        payc = call(
            functools.partial(grow_kernel, n, blk, chooser), shaped(2 * n + 2 * blk, nvec, BF16), payc, gotc
        )
        n *= 2
    gotc = send(payc, core_hop, core_hop)
    projected = call(functools.partial(final_kernel, n, blk, scale), shaped(nvec, nvec, F32), payc, gotc)

    def back(x):
        return jnp.transpose(x.reshape(modes_here, nb, nvec), (1, 0, 2))

    return projected, back(turned_basis), back(turned_images)


def solution(mesh):
    placed = (
        P("site", "mode", None),
        P("site", "mode", None),
        P("site", None, "mode", None),
        P("site", None),
        P(),
    )
    return jax.shard_map(
        program,
        mesh=mesh,
        in_specs=placed,
        out_specs=(P(), P("site", "mode", None), P("site", "mode", None)),
        check_vma=False,
    )
```

```python
import functools
import math

import jax
import jax.numpy as jnp
from jax import lax
from jax.experimental import pallas as pl
from jax.experimental.pallas import tpu as pltpu
from jax.sharding import PartitionSpec as P


F32 = jnp.float32
BF16 = jnp.bfloat16
BOTH = ("site", "mode")
LANES = 128
PIECES = 5


def dot_nn(a, b):
    return lax.dot_general(a, b, (((1,), (0,)), ((), ())), preferred_element_type=F32)


def dot_tn(a, b):
    return lax.dot_general(a, b, (((0,), (0,)), ((), ())), preferred_element_type=F32)


def onehot(shape, test):
    rows = lax.broadcasted_iota(jnp.int32, shape, 0)
    cols = lax.broadcasted_iota(jnp.int32, shape, 1)
    return jnp.where(test(rows, cols), 1.0, 0.0).astype(BF16)


def split(x):
    high = x.astype(BF16)
    low = (x - high.astype(F32)).astype(BF16)
    return high, low


def place():
    mode = lax.axis_index("mode")
    site = lax.axis_index("site")
    core = lax.rem(mode, 2)
    half = lax.div(mode, 2)
    y = lax.rem(site, 2)
    z0 = lax.rem(lax.div(site, 2), 2)
    z1 = lax.rem(lax.div(site, 4), 2)
    return core, half, y, z0, z1


def pick(core, first, second):
    return first * (1 - core) + second * core


def rows_at(index, count):
    return pl.ds(pl.multiple_of(index * count, count), count)


def call(kernel, outs, *args, scratch=(), flops=10**8, moved=2 * 10**6, smem=(), far=(), out_far=False):
    vmem = pl.BlockSpec(memory_space=pltpu.VMEM)
    scalars = pl.BlockSpec(memory_space=pltpu.SMEM)
    distant = pl.BlockSpec(memory_space=pltpu.HBM)
    return pl.pallas_call(
        kernel,
        out_shape=outs,
        in_specs=[scalars if i in smem else distant if i in far else vmem for i in range(len(args))],
        out_specs=jax.tree.map(lambda _: pl.BlockSpec(memory_space=pl.ANY) if out_far else vmem, outs),
        scratch_shapes=scratch,
        compiler_params=pltpu.CompilerParams(vmem_limit_bytes=16 * 2**20),
        cost_estimate=pl.CostEstimate(flops=flops, bytes_accessed=moved, transcendentals=0),
    )(*args)


def stay(x):
    return pltpu.with_memory_space_constraint(x, pltpu.HBM)


def shaped(rows, cols, dtype):
    return jax.ShapeDtypeStruct((rows, cols), dtype)


def open_kernel(nb, spots, basis_far, images_far, pay, basis, images, shift, sems):
    rows, nvec = basis.shape
    old = images.shape[1]
    blk = nvec - old
    step = rows // PIECES
    copies = []
    for j, (far, here) in enumerate(((basis_far, basis), (images_far, images))):
        for i in range(PIECES):
            span = pl.ds(i * step, step)
            copies.append(pltpu.make_async_copy(far.at[span], here.at[span], sems.at[j * PIECES + i]))
    for copy in copies:
        copy.start()
    core = place()[0]
    top = nvec // 2
    wide = nb * blk
    share = shift.shape[0] // spots
    shift[...] = onehot(
        shift.shape,
        lambda r, c: (lax.rem(c, LANES) < share) & (lax.div(c, LANES) * share + lax.rem(c, LANES) == r),
    )
    gather = onehot((LANES, rows), lambda r, c: lax.div(c, nb) == r)
    spread = onehot((LANES, wide), lambda r, c: r - (LANES - blk) == lax.rem(c, blk))
    for copy in copies[:PIECES]:
        copy.wait()
    tiled = dot_nn(basis[:, nvec - LANES :], spread)
    row = lax.broadcasted_iota(jnp.int32, (rows, wide), 0)
    col = lax.broadcasted_iota(jnp.int32, (rows, wide), 1)
    tiled = jnp.where(lax.rem(row, nb) == lax.div(col, blk), tiled, 0.0).astype(BF16)
    merged = dot_nn(gather, tiled).astype(BF16)
    groups = nvec // LANES
    each = LANES // groups
    for g in range(groups):
        pay[2 * top :, g * LANES : (g + 1) * LANES] = merged[g * each : (g + 1) * each]
    for copy in copies[PIECES:]:
        copy.wait()
    give = basis[:, pl.ds(pl.multiple_of((1 - core) * top, top), top)]
    high, low = split(dot_tn(give, images[...]))
    pay[:top, :old] = high
    pay[:top, old:] = jnp.zeros((top, blk), BF16)
    pay[top : 2 * top, :old] = low
    pay[top : 2 * top, old:] = jnp.zeros((top, blk), BF16)


def fetch_kernel(order, far, near, sems):
    copies = [pltpu.make_async_copy(far.at[hop], near.at[i], sems.at[i]) for i, hop in enumerate(order)]
    for copy in copies:
        copy.start()
    for copy in copies:
        copy.wait()


def keep_kernel(basis, images, kept):
    nvec = basis.shape[1]
    old = images.shape[1]
    core = place()[0]
    top = nvec // 2
    mine = basis[:, pl.ds(pl.multiple_of(core * top, top), top)]
    kept[:, :old] = dot_tn(mine, images[...])
    kept[:, old:] = jnp.zeros((top, nvec - old), F32)


def put(far, held, sems, pieces, work):
    step = held.shape[0] // pieces
    copies = []
    for i in range(pieces):
        span = pl.ds(i * step, step)
        held[span, :] = work(span)
        copy = pltpu.make_async_copy(held.at[span], far.at[span], sems.at[i])
        copy.start()
        copies.append(copy)
    for copy in copies:
        copy.wait()


def rotate_kernel(basis, rotation, far, held, sems):
    put(far, held, sems, PIECES, lambda span: dot_nn(basis[span, :], rotation[...]).astype(BF16))


def joined(kept, got, start, count):
    whole = kept.shape[0]
    rows = pl.ds(pl.multiple_of(start, count), count)
    lows = pl.ds(pl.multiple_of(start + whole, count), count)
    return kept[rows, :] + (got[rows, :].astype(F32) + got[lows, :].astype(F32))


def second_kernel(kept, got, pay, out, rest, pair):
    core, half, y, _, _ = place()
    whole = kept.shape[0]
    n = whole // 2
    bit = pick(core, half, y)
    out[:n, :], out[n : 2 * n, :] = split(joined(kept, got, (1 - bit) * n, n))
    rest[...] = joined(kept, got, bit * n, n)
    each = got.shape[0] - 2 * whole
    pair[rows_at(core, each), :] = pay[2 * whole :, :]
    pair[rows_at(1 - core, each), :] = got[2 * whole :, :]
    out[2 * n :, :] = pair[...]


def third_kernel(kept, got, pair, far, out, rest):
    core, half, _, z0, _ = place()
    whole = kept.shape[0]
    n = whole // 2
    bit = pick(core, z0, half)
    out[:n, :], out[n : 2 * n, :] = split(joined(kept, got, (1 - bit) * n, n))
    rest[...] = joined(kept, got, bit * n, n)
    each = pair.shape[0]
    at = pick(core, 1 - half, 0)
    out[pl.ds(pl.multiple_of(2 * n + at * each, each), each), :] = got[2 * whole :, :]
    out[pl.ds(pl.multiple_of(2 * n + (1 - at) * each, each), each), :] = jnp.where(
        core == 0, pair[...], far[...]
    )


def fourth_kernel(kept, got, far, out, rest, cross):
    core, _, y, _, z1 = place()
    whole = kept.shape[0]
    n = whole // 2
    bit = pick(core, y, z1)
    out[:n, :], out[n:, :] = split(joined(kept, got, (1 - bit) * n, n))
    rest[...] = joined(kept, got, bit * n, n)
    area = got.shape[0] - 2 * whole
    cross[:area, :] = got[2 * whole :, :]
    cross[area:, :] = far[...]


def setup_kernel(near, nb, blk, table, perms):
    hops = perms.shape[0]
    wide = nb * blk
    row = lax.broadcasted_iota(jnp.int32, (2 * wide, wide), 0)
    col = lax.broadcasted_iota(jnp.int32, (1, wide), 1)
    for hop in range(hops):
        wanted = col if hop == 0 else lax.rem(col, blk)
        for b in range(nb if hop else 0):
            entry = table[b, hop - 1]
            base = lax.rem(entry, nb) * blk
            if hop not in near:
                base = base + jnp.where(entry >= nb, wide, 0)
            wanted = wanted + jnp.where(lax.div(col, blk) == b, base, 0)
        perms[hop] = jnp.where(row == wanted, 1.0, 0.0).astype(BF16)


def stack(ref, at, piece):
    rows, nvec = piece.shape
    groups = nvec // LANES
    each = LANES // groups
    chunks = rows // each
    parts = [
        piece[m * each : (m + 1) * each, g * LANES : (g + 1) * LANES] for m in range(chunks) for g in range(groups)
    ]
    ref[rows_at(at, chunks * LANES), :] = jnp.concatenate(parts, axis=0)


def near_kernel(order, pair, got, crossed, hops, perms, shift, total, own_out, column):
    core, half, _, _, _ = place()
    each = pair.shape[0]
    wide = own_out.shape[1]
    area = got.shape[0]
    stack(column, half, pair[...])
    stack(column, 1 - half, jnp.where(core == 0, got[area - each :, :], crossed[...]))
    own = dot_nn(shift[...], column[...]).astype(BF16)
    own_out[...] = own
    rows = total.shape[0]
    mixed = [dot_nn(own, perms[hop, :wide, :]).astype(BF16) for hop in order]
    step = rows // 2
    for r in range(2):
        span = pl.ds(r * step, step)
        part = dot_nn(hops[0, span, :], mixed[0])
        for i in range(1, len(order)):
            part = part + dot_nn(hops[i, span, :], mixed[i])
        total[span, :] = part


def far_kernel(nb, blk, own, got2, cross, far, got1, crossed, total, basis, hops, perms, shift, *refs):
    times, (masked, new_out, column) = refs[:-3], refs[-3:]
    core, half, _, _, _ = place()
    each = far.shape[0]
    wide = own.shape[1]
    rows = basis.shape[0]
    nvec = basis.shape[1]
    first = core == 0
    mine = got2[got2.shape[0] - 2 * each :, :]
    theirs = cross[: 2 * each, :]
    sites = []
    one = jnp.where(first, theirs, mine)
    two = jnp.where(first, mine, theirs)
    stack(column.at[0], half, jnp.where(first, crossed[...], got1[got1.shape[0] - each :, :]))
    stack(column.at[0], 1 - half, one[:each])
    stack(column.at[1], half, jnp.where(first, cross[2 * each :, :], far[...]))
    stack(column.at[1], 1 - half, one[each:])
    stack(column.at[2], 0, two)
    near_site = dot_nn(shift[...], column[0]).astype(BF16)
    long_site = dot_nn(shift[...], column[1]).astype(BF16)
    mid_site = dot_nn(shift[...], column[2]).astype(BF16)
    sites = {1: long_site, 4: long_site, 2: mid_site, 5: mid_site, 3: near_site, 6: near_site}
    for k, ref in enumerate(times):
        sites[7 + k] = ref[...]
    order = sorted(sites)
    mixed = [
        dot_nn(jnp.concatenate([own[...], sites[hop]], axis=1), perms[hop]).astype(BF16) for hop in order
    ]
    step = rows // 2
    sums = jnp.zeros((wide, nvec), F32)
    for r in range(2):
        span = pl.ds(r * step, step)
        part = total[span, :]
        for i in range(len(order)):
            part = part + dot_nn(hops[i, span, :], mixed[i])
        row = lax.broadcasted_iota(jnp.int32, (step, wide), 0)
        col = lax.broadcasted_iota(jnp.int32, (step, wide), 1)
        chosen = jnp.where(lax.rem(row, nb) == lax.div(col, blk), part, 0.0).astype(BF16)
        masked[span, :] = chosen
        sums = sums + dot_tn(chosen, basis[span, :])
    new = sums[:blk]
    for b in range(1, nb):
        new = new + sums[b * blk : (b + 1) * blk]
    new_out[:blk, :], new_out[blk:, :] = split(new)


def join_kernel(kept, got, new, out):
    n = kept.shape[0]
    total = kept[...] + (got[:n, :].astype(F32) + got[n:, :].astype(F32))
    out[:n, :], out[n : 2 * n, :] = split(total)
    out[2 * n :, :] = new[...]


def turn_kernel(nb, images, masked, rotation, far, held, sems):
    old = images.shape[1]
    tail = rotation[old:, :]
    deep = jnp.concatenate([tail] * nb, axis=0)
    put(
        far,
        held,
        sems,
        PIECES,
        lambda span: (dot_nn(images[span, :], rotation[:old, :]) + dot_nn(masked[span, :], deep)).astype(BF16),
    )


def value(ref, start, count):
    return ref[start : start + count, :].astype(F32) + ref[start + count : start + 2 * count, :].astype(F32)


def extra_kernel(n, blk, pay, got, out):
    out[:n, :], out[n : 2 * n, :] = split(value(pay, 0, n) + value(got, 0, n))
    out[2 * n : 2 * n + blk, :], out[2 * n + blk :, :] = split(value(pay, 2 * n, blk) + value(got, 2 * n, blk))


def settle_kernel(n, blk, scale, pay, got, out):
    out[:n, :] = ((value(pay, 0, n) + value(got, 0, n)) * scale).astype(BF16)
    out[n : n + blk, :], out[n + blk :, :] = split(value(pay, 2 * n, blk) + value(got, 2 * n, blk))


def grow_kernel(n, blk, chooser, pay, got, out):
    bit = chooser(*place())
    out[rows_at(bit, n), :] = pay[:n, :]
    out[rows_at(1 - bit, n), :] = got[:n, :]
    out[2 * n : 2 * n + blk, :], out[2 * n + blk :, :] = split(value(pay, n, blk) + value(got, n, blk))


def final_kernel(n, blk, scale, pay, got, far, held, sems):
    nvec = far.shape[1]
    core = place()[0]
    new = (value(pay, n, blk) + value(got, n, blk)) * scale
    tall = jnp.concatenate([jnp.zeros((LANES - blk, nvec), F32), new], axis=0)
    held[:, nvec - LANES :] = tall.T
    step = n // 2
    lane = lax.broadcasted_iota(jnp.int32, (step, LANES), 1)
    copies = []
    for i in range(4):
        side = core if i < 2 else 1 - core
        source = pay if i < 2 else got
        part = source[(i % 2) * step : (i % 2 + 1) * step, :].astype(F32)
        span = pl.ds(pl.multiple_of(side * n + (i % 2) * step, step), step)
        held[span, : nvec - LANES] = part[:, : nvec - LANES]
        held[span, nvec - LANES :] = jnp.where(
            lane < LANES - blk, part[:, nvec - LANES :], held[span, nvec - LANES :]
        )
        copy = pltpu.make_async_copy(held.at[span], far.at[span], sems.at[i])
        copy.start()
        copies.append(copy)
    for copy in copies:
        copy.wait()


def program(basis, images, hops, neighbours, rotation):
    nb, modes_here, nvec = basis.shape
    old = images.shape[2]
    blk = nvec - old
    sites = lax.axis_size("site")
    spots = lax.axis_size("mode")
    count = sites * spots
    rows = nb * modes_here
    coarse = hops.shape[3]
    wide = nb * blk
    chunk = wide * LANES // nvec
    scale = 1.0 / math.sqrt(count * rows)

    def send(x, first, second):
        pairs = [(d, d ^ hop) for d in range(count) for hop in [second if d % 2 else first] if hop]
        return lax.ppermute(x, BOTH, pairs)

    core_hop, x_hop, y_hop, z0_hop, z1_hop = 1, 2, spots, 2 * spots, 4 * spots

    flat_basis = jnp.transpose(basis, (1, 0, 2)).reshape(rows, nvec)
    flat_images = jnp.transpose(images, (1, 0, 2)).reshape(rows, old)
    flat_hops = jnp.transpose(hops, (1, 2, 0, 3)).reshape(hops.shape[1], rows, coarse)
    half = nvec // 2
    n = half // 8
    pay0, basis_here, images_here, shift = call(
        functools.partial(open_kernel, nb, spots),
        (
            shaped(nvec + chunk, nvec, BF16),
            shaped(rows, nvec, BF16),
            shaped(rows, old, BF16),
            shaped(coarse, spots * LANES, BF16),
        ),
        stay(flat_basis),
        stay(flat_images),
        far=(0, 1),
        scratch=[pltpu.SemaphoreType.DMA((2 * PIECES,))],
    )
    got0 = send(pay0, core_hop, core_hop)
    kept0 = call(keep_kernel, shaped(half, nvec, F32), basis_here, images_here)
    near_order = [0] if sites > 8 else [0, 7, 8]
    far_order = [hop for hop in range(hops.shape[1]) if hop not in near_order]

    def fetched(order):
        return call(
            functools.partial(fetch_kernel, order),
            jax.ShapeDtypeStruct((len(order), rows, coarse), BF16),
            stay(flat_hops),
            far=(0,),
            scratch=[pltpu.SemaphoreType.DMA((len(order),))],
        )

    far_hops = fetched(far_order)
    near_hops = fetched(near_order)
    perms = call(
        functools.partial(setup_kernel, near_order, nb, blk),
        jax.ShapeDtypeStruct((hops.shape[1], 2 * wide, wide), BF16),
        neighbours,
        smem=(0,),
    )
    pay1, kept1, pair = call(
        second_kernel,
        (shaped(half + 2 * chunk, nvec, BF16), shaped(half // 2, nvec, F32), shaped(2 * chunk, nvec, BF16)),
        kept0,
        got0,
        pay0,
    )
    got1 = send(pay1, x_hop, y_hop)
    far = send(pair, 0, z1_hop)
    pay2, kept2 = call(
        third_kernel,
        (shaped(half // 2 + 4 * chunk, nvec, BF16), shaped(half // 4, nvec, F32)),
        kept1,
        got1,
        pair,
        far,
    )
    got2 = send(pay2, z0_hop, x_hop)
    crossed = send(got1[half:, :], core_hop, core_hop)
    total, own = call(
        functools.partial(near_kernel, near_order),
        (shaped(rows, wide, F32), shaped(coarse, wide, BF16)),
        pair,
        got1,
        crossed,
        near_hops,
        perms,
        shift,
        scratch=[pltpu.VMEM((spots * LANES, wide), BF16)],
    )
    times = []
    if sites > 8:
        gap = 8 * spots
        times = [lax.ppermute(own, BOTH, [((d + sign * gap) % count, d) for d in range(count)]) for sign in (1, -1)]
    pay3, kept3, cross_pay = call(
        fourth_kernel,
        (shaped(half // 4, nvec, BF16), shaped(half // 8, nvec, F32), shaped(6 * chunk, nvec, BF16)),
        kept2,
        got2,
        far,
    )
    cross = send(cross_pay, core_hop, core_hop)
    got3 = send(pay3, y_hop, z1_hop)
    masked, new = call(
        functools.partial(far_kernel, nb, blk),
        (shaped(rows, wide, BF16), shaped(2 * blk, nvec, BF16)),
        own,
        got2,
        cross,
        far,
        got1,
        crossed,
        total,
        basis_here,
        far_hops,
        perms,
        shift,
        *times,
        scratch=[pltpu.VMEM((3, spots * LANES, wide), BF16)],
    )
    payc = call(join_kernel, shaped(2 * n + 2 * blk, nvec, BF16), kept3, got3, new)
    turned = [pltpu.VMEM((rows, nvec), BF16), pltpu.SemaphoreType.DMA((PIECES,))]
    gotc = send(payc, z1_hop, z0_hop)
    turned_images = call(
        functools.partial(turn_kernel, nb),
        shaped(rows, nvec, BF16),
        images_here,
        masked,
        rotation,
        out_far=True,
        scratch=turned,
    )
    hop = 8 * spots
    while hop < count:
        payc = call(functools.partial(extra_kernel, n, blk), shaped(2 * n + 2 * blk, nvec, BF16), payc, gotc)
        gotc = send(payc, hop, hop)
        hop *= 2
    payc = call(functools.partial(settle_kernel, n, blk, scale), shaped(n + 2 * blk, nvec, BF16), payc, gotc)
    steps = (
        (y_hop, z1_hop, lambda core, half, y, z0, z1: pick(core, y, z1)),
        (z0_hop, x_hop, lambda core, half, y, z0, z1: pick(core, z0, half)),
        (x_hop, y_hop, lambda core, half, y, z0, z1: pick(core, half, y)),
    )
    turned_basis = call(
        rotate_kernel, shaped(rows, nvec, BF16), basis_here, rotation, out_far=True, scratch=turned
    )
    for first, second, chooser in steps:
        gotc = send(payc, first, second)
        payc = call(
            functools.partial(grow_kernel, n, blk, chooser), shaped(2 * n + 2 * blk, nvec, BF16), payc, gotc
        )
        n *= 2
    gotc = send(payc, core_hop, core_hop)
    projected = call(
        functools.partial(final_kernel, n, blk, scale),
        shaped(nvec, nvec, F32),
        payc,
        gotc,
        out_far=True,
        scratch=[pltpu.VMEM((nvec, nvec), F32), pltpu.SemaphoreType.DMA((4,))],
    )

    def back(x):
        return jnp.transpose(x.reshape(modes_here, nb, nvec), (1, 0, 2))

    return projected, back(turned_basis), back(turned_images)


def solution(mesh):
    placed = (
        P("site", "mode", None),
        P("site", "mode", None),
        P("site", None, "mode", None),
        P("site", None),
        P(),
    )
    return jax.shard_map(
        program,
        mesh=mesh,
        in_specs=placed,
        out_specs=(P(), P("site", "mode", None), P("site", "mode", None)),
        check_vma=False,
    )
```

```python
import functools
import math

import jax
import jax.numpy as jnp
from jax import lax
from jax.experimental import pallas as pl
from jax.experimental.pallas import tpu as pltpu
from jax.sharding import PartitionSpec as P


F32 = jnp.float32
BF16 = jnp.bfloat16
BOTH = ("site", "mode")
LANES = 128
PIECES = 5


def dot_nn(a, b):
    return lax.dot_general(a, b, (((1,), (0,)), ((), ())), preferred_element_type=F32)


def dot_tn(a, b):
    return lax.dot_general(a, b, (((0,), (0,)), ((), ())), preferred_element_type=F32)


def onehot(shape, test):
    rows = lax.broadcasted_iota(jnp.int32, shape, 0)
    cols = lax.broadcasted_iota(jnp.int32, shape, 1)
    return jnp.where(test(rows, cols), 1.0, 0.0).astype(BF16)


def split(x):
    high = x.astype(BF16)
    low = (x - high.astype(F32)).astype(BF16)
    return high, low


def place():
    mode = lax.axis_index("mode")
    site = lax.axis_index("site")
    core = lax.rem(mode, 2)
    half = lax.div(mode, 2)
    y = lax.rem(site, 2)
    z0 = lax.rem(lax.div(site, 2), 2)
    z1 = lax.rem(lax.div(site, 4), 2)
    return core, half, y, z0, z1


def pick(core, first, second):
    return first * (1 - core) + second * core


def rows_at(index, count):
    return pl.ds(pl.multiple_of(index * count, count), count)


def call(kernel, outs, *args, scratch=(), flops=10**8, moved=2 * 10**6, smem=(), far=(), out_far=False):
    vmem = pl.BlockSpec(memory_space=pltpu.VMEM)
    scalars = pl.BlockSpec(memory_space=pltpu.SMEM)
    distant = pl.BlockSpec(memory_space=pltpu.HBM)
    return pl.pallas_call(
        kernel,
        out_shape=outs,
        in_specs=[scalars if i in smem else distant if i in far else vmem for i in range(len(args))],
        out_specs=jax.tree.map(lambda _: pl.BlockSpec(memory_space=pl.ANY) if out_far else vmem, outs),
        scratch_shapes=scratch,
        compiler_params=pltpu.CompilerParams(vmem_limit_bytes=16 * 2**20),
        cost_estimate=pl.CostEstimate(flops=flops, bytes_accessed=moved, transcendentals=0),
    )(*args)


def stay(x):
    return pltpu.with_memory_space_constraint(x, pltpu.HBM)


def shaped(rows, cols, dtype):
    return jax.ShapeDtypeStruct((rows, cols), dtype)


def open_kernel(nb, spots, near, basis_far, images_far, table_far, hops_far, pay, basis, images, shift, perms, hops, table, sems):
    rows, nvec = basis.shape
    old = images.shape[1]
    blk = nvec - old
    step = rows // PIECES
    copies = []
    for j, (far, here) in enumerate(((basis_far, basis), (images_far, images))):
        for i in range(PIECES):
            span = pl.ds(i * step, step)
            copies.append(pltpu.make_async_copy(far.at[span], here.at[span], sems.at[j * PIECES + i]))
    small = pltpu.make_async_copy(table_far, table, sems.at[2 * PIECES])
    small.start()
    for i, hop in enumerate(near):
        copies.append(pltpu.make_async_copy(hops_far.at[hop], hops.at[i], sems.at[2 * PIECES + 1 + i]))
    for copy in copies:
        copy.start()
    core = place()[0]
    top = nvec // 2
    wide = nb * blk
    share = shift.shape[0] // spots
    shift[...] = onehot(
        shift.shape,
        lambda r, c: (lax.rem(c, LANES) < share) & (lax.div(c, LANES) * share + lax.rem(c, LANES) == r),
    )
    gather = onehot((LANES, rows), lambda r, c: lax.div(c, nb) == r)
    spread = onehot((LANES, wide), lambda r, c: r - (LANES - blk) == lax.rem(c, blk))
    small.wait()
    choose(near, nb, blk, table[...], perms)
    for copy in copies[:PIECES]:
        copy.wait()
    tiled = dot_nn(basis[:, nvec - LANES :], spread)
    row = lax.broadcasted_iota(jnp.int32, (rows, wide), 0)
    col = lax.broadcasted_iota(jnp.int32, (rows, wide), 1)
    tiled = jnp.where(lax.rem(row, nb) == lax.div(col, blk), tiled, 0.0).astype(BF16)
    merged = dot_nn(gather, tiled).astype(BF16)
    groups = nvec // LANES
    each = LANES // groups
    for g in range(groups):
        pay[2 * top :, g * LANES : (g + 1) * LANES] = merged[g * each : (g + 1) * each]
    for copy in copies[PIECES : 2 * PIECES]:
        copy.wait()
    give = basis[:, pl.ds(pl.multiple_of((1 - core) * top, top), top)]
    high, low = split(dot_tn(give, images[...]))
    pay[:top, :old] = high
    pay[:top, old:] = jnp.zeros((top, blk), BF16)
    pay[top : 2 * top, :old] = low
    pay[top : 2 * top, old:] = jnp.zeros((top, blk), BF16)
    for copy in copies[2 * PIECES :]:
        copy.wait()


def fetch_kernel(order, far, near, sems):
    copies = [pltpu.make_async_copy(far.at[hop], near.at[i], sems.at[i]) for i, hop in enumerate(order)]
    for copy in copies:
        copy.start()
    for copy in copies:
        copy.wait()


def keep_kernel(basis, images, kept):
    nvec = basis.shape[1]
    old = images.shape[1]
    core = place()[0]
    top = nvec // 2
    mine = basis[:, pl.ds(pl.multiple_of(core * top, top), top)]
    kept[:, :old] = dot_tn(mine, images[...])
    kept[:, old:] = jnp.zeros((top, nvec - old), F32)


def put(far, held, sems, pieces, work):
    step = held.shape[0] // pieces
    copies = []
    for i in range(pieces):
        span = pl.ds(i * step, step)
        held[span, :] = work(span)
        copy = pltpu.make_async_copy(held.at[span], far.at[span], sems.at[i])
        copy.start()
        copies.append(copy)
    for copy in copies:
        copy.wait()


def rotate_kernel(basis, rotation, far, held, sems):
    put(far, held, sems, PIECES, lambda span: dot_nn(basis[span, :], rotation[...]).astype(BF16))


def joined(kept, got, start, count):
    whole = kept.shape[0]
    rows = pl.ds(pl.multiple_of(start, count), count)
    lows = pl.ds(pl.multiple_of(start + whole, count), count)
    return kept[rows, :] + (got[rows, :].astype(F32) + got[lows, :].astype(F32))


def second_kernel(kept, got, pay, out, rest, pair):
    core, half, y, _, _ = place()
    whole = kept.shape[0]
    n = whole // 2
    bit = pick(core, half, y)
    out[:n, :], out[n : 2 * n, :] = split(joined(kept, got, (1 - bit) * n, n))
    rest[...] = joined(kept, got, bit * n, n)
    each = got.shape[0] - 2 * whole
    pair[rows_at(core, each), :] = pay[2 * whole :, :]
    pair[rows_at(1 - core, each), :] = got[2 * whole :, :]
    out[2 * n :, :] = pair[...]


def third_kernel(kept, got, pair, far, out, rest):
    core, half, _, z0, _ = place()
    whole = kept.shape[0]
    n = whole // 2
    bit = pick(core, z0, half)
    out[:n, :], out[n : 2 * n, :] = split(joined(kept, got, (1 - bit) * n, n))
    rest[...] = joined(kept, got, bit * n, n)
    each = pair.shape[0]
    at = pick(core, 1 - half, 0)
    out[pl.ds(pl.multiple_of(2 * n + at * each, each), each), :] = got[2 * whole :, :]
    out[pl.ds(pl.multiple_of(2 * n + (1 - at) * each, each), each), :] = jnp.where(
        core == 0, pair[...], far[...]
    )


def fourth_kernel(kept, got, far, out, rest, cross):
    core, _, y, _, z1 = place()
    whole = kept.shape[0]
    n = whole // 2
    bit = pick(core, y, z1)
    out[:n, :], out[n:, :] = split(joined(kept, got, (1 - bit) * n, n))
    rest[...] = joined(kept, got, bit * n, n)
    area = got.shape[0] - 2 * whole
    cross[:area, :] = got[2 * whole :, :]
    cross[area:, :] = far[...]


def choose(near, nb, blk, table, perms):
    hops = perms.shape[0]
    wide = nb * blk
    row = lax.broadcasted_iota(jnp.int32, (2 * wide, wide), 0)
    col = lax.broadcasted_iota(jnp.int32, (hops - 1, wide), 1)
    repeat = onehot((nb, wide), lambda r, c: lax.div(c, blk) == r)
    entry = dot_tn(table.astype(F32).astype(BF16), repeat).astype(jnp.int32)
    piece = lax.div(entry, nb)
    wanted = (entry - piece * nb) * blk + lax.rem(col, blk)
    aside = wanted + jnp.where(piece > 0, wide, 0)
    perms[0] = onehot((2 * wide, wide), lambda r, c: r == c)
    for hop in range(1, hops):
        target = (wanted if hop in near else aside)[hop - 1 : hop, :]
        perms[hop] = jnp.where(row == target, 1.0, 0.0).astype(BF16)


def stack(ref, at, piece):
    rows, nvec = piece.shape
    groups = nvec // LANES
    each = LANES // groups
    chunks = rows // each
    parts = [
        piece[m * each : (m + 1) * each, g * LANES : (g + 1) * LANES] for m in range(chunks) for g in range(groups)
    ]
    ref[rows_at(at, chunks * LANES), :] = jnp.concatenate(parts, axis=0)


def near_kernel(order, pair, got, crossed, hops, perms, shift, total, own_out, column):
    core, half, _, _, _ = place()
    each = pair.shape[0]
    wide = own_out.shape[1]
    area = got.shape[0]
    stack(column, half, pair[...])
    stack(column, 1 - half, jnp.where(core == 0, got[area - each :, :], crossed[...]))
    own = dot_nn(shift[...], column[...]).astype(BF16)
    own_out[...] = own
    rows = total.shape[0]
    mixed = [dot_nn(own, perms[hop, :wide, :]).astype(BF16) for hop in order]
    step = rows // 2
    for r in range(2):
        span = pl.ds(r * step, step)
        part = dot_nn(hops[0, span, :], mixed[0])
        for i in range(1, len(order)):
            part = part + dot_nn(hops[i, span, :], mixed[i])
        total[span, :] = part


def far_kernel(nb, blk, own, got2, cross, far, got1, crossed, total, basis, hops, more, perms, shift, *refs):
    times, (masked, new_out, column) = refs[:-3], refs[-3:]
    core, half, _, _, _ = place()
    each = far.shape[0]
    wide = own.shape[1]
    rows = basis.shape[0]
    nvec = basis.shape[1]
    first = core == 0
    mine = got2[got2.shape[0] - 2 * each :, :]
    theirs = cross[: 2 * each, :]
    sites = []
    one = jnp.where(first, theirs, mine)
    two = jnp.where(first, mine, theirs)
    stack(column.at[0], half, jnp.where(first, crossed[...], got1[got1.shape[0] - each :, :]))
    stack(column.at[0], 1 - half, one[:each])
    stack(column.at[1], half, jnp.where(first, cross[2 * each :, :], far[...]))
    stack(column.at[1], 1 - half, one[each:])
    stack(column.at[2], 0, two)
    near_site = dot_nn(shift[...], column[0]).astype(BF16)
    long_site = dot_nn(shift[...], column[1]).astype(BF16)
    mid_site = dot_nn(shift[...], column[2]).astype(BF16)
    sites = {1: long_site, 4: long_site, 2: mid_site, 5: mid_site, 3: near_site, 6: near_site}
    for k, ref in enumerate(times):
        sites[7 + k] = ref[...]
    order = sorted(sites)
    mixed = [
        dot_nn(jnp.concatenate([own[...], sites[hop]], axis=1), perms[hop]).astype(BF16) for hop in order
    ]
    step = rows // 2
    sums = jnp.zeros((wide, nvec), F32)
    for r in range(2):
        span = pl.ds(r * step, step)
        part = total[span, :]
        for i in range(len(order)):
            source = hops if i < hops.shape[0] else more
            part = part + dot_nn(source[i % hops.shape[0], span, :], mixed[i])
        row = lax.broadcasted_iota(jnp.int32, (step, wide), 0)
        col = lax.broadcasted_iota(jnp.int32, (step, wide), 1)
        chosen = jnp.where(lax.rem(row, nb) == lax.div(col, blk), part, 0.0).astype(BF16)
        masked[span, :] = chosen
        sums = sums + dot_tn(chosen, basis[span, :])
    new = sums[:blk]
    for b in range(1, nb):
        new = new + sums[b * blk : (b + 1) * blk]
    new_out[:blk, :], new_out[blk:, :] = split(new)


def join_kernel(kept, got, new, out):
    n = kept.shape[0]
    total = kept[...] + (got[:n, :].astype(F32) + got[n:, :].astype(F32))
    out[:n, :], out[n : 2 * n, :] = split(total)
    out[2 * n :, :] = new[...]


def turn_kernel(nb, images, masked, rotation, far, held, sems):
    old = images.shape[1]
    tail = rotation[old:, :]
    deep = jnp.concatenate([tail] * nb, axis=0)
    put(
        far,
        held,
        sems,
        PIECES,
        lambda span: (dot_nn(images[span, :], rotation[:old, :]) + dot_nn(masked[span, :], deep)).astype(BF16),
    )


def value(ref, start, count):
    return ref[start : start + count, :].astype(F32) + ref[start + count : start + 2 * count, :].astype(F32)


def extra_kernel(n, blk, pay, got, out):
    out[:n, :], out[n : 2 * n, :] = split(value(pay, 0, n) + value(got, 0, n))
    out[2 * n : 2 * n + blk, :], out[2 * n + blk :, :] = split(value(pay, 2 * n, blk) + value(got, 2 * n, blk))


def settle_kernel(n, blk, scale, pay, got, out):
    out[:n, :] = ((value(pay, 0, n) + value(got, 0, n)) * scale).astype(BF16)
    out[n : n + blk, :], out[n + blk :, :] = split(value(pay, 2 * n, blk) + value(got, 2 * n, blk))


def grow_kernel(n, blk, chooser, pay, got, out):
    bit = chooser(*place())
    out[rows_at(bit, n), :] = pay[:n, :]
    out[rows_at(1 - bit, n), :] = got[:n, :]
    out[2 * n : 2 * n + blk, :], out[2 * n + blk :, :] = split(value(pay, n, blk) + value(got, n, blk))


def join_four_kernel(n, blk, first, second, pay, got_a, got_b, got_ab, out):
    spot = place()
    a, b = first(*spot), second(*spot)
    out[rows_at(2 * b + a, n), :] = pay[:n, :]
    out[rows_at(2 * b + 1 - a, n), :] = got_a[:n, :]
    out[rows_at(2 * (1 - b) + a, n), :] = got_b[:n, :]
    out[rows_at(2 * (1 - b) + 1 - a, n), :] = got_ab[:n, :]
    new = (value(pay, n, blk) + value(got_a, n, blk)) + (value(got_b, n, blk) + value(got_ab, n, blk))
    out[4 * n : 4 * n + blk, :], out[4 * n + blk :, :] = split(new)


def final_kernel(n, blk, scale, pay, got, far, held, sems):
    nvec = far.shape[1]
    core = place()[0]
    new = (value(pay, n, blk) + value(got, n, blk)) * scale
    tall = jnp.concatenate([jnp.zeros((LANES - blk, nvec), F32), new], axis=0)
    held[:, nvec - LANES :] = tall.T
    step = n // 2
    lane = lax.broadcasted_iota(jnp.int32, (step, LANES), 1)
    copies = []
    for i in range(4):
        side = core if i < 2 else 1 - core
        source = pay if i < 2 else got
        part = source[(i % 2) * step : (i % 2 + 1) * step, :].astype(F32)
        span = pl.ds(pl.multiple_of(side * n + (i % 2) * step, step), step)
        held[span, : nvec - LANES] = part[:, : nvec - LANES]
        held[span, nvec - LANES :] = jnp.where(
            lane < LANES - blk, part[:, nvec - LANES :], held[span, nvec - LANES :]
        )
        copy = pltpu.make_async_copy(held.at[span], far.at[span], sems.at[i])
        copy.start()
        copies.append(copy)
    for copy in copies:
        copy.wait()


def program(basis, images, hops, neighbours, rotation):
    nb, modes_here, nvec = basis.shape
    old = images.shape[2]
    blk = nvec - old
    sites = lax.axis_size("site")
    spots = lax.axis_size("mode")
    count = sites * spots
    rows = nb * modes_here
    coarse = hops.shape[3]
    wide = nb * blk
    chunk = wide * LANES // nvec
    scale = 1.0 / math.sqrt(count * rows)

    def send(x, first, second):
        pairs = [(d, d ^ hop) for d in range(count) for hop in [second if d % 2 else first] if hop]
        return lax.ppermute(x, BOTH, pairs)

    core_hop, x_hop, y_hop, z0_hop, z1_hop = 1, 2, spots, 2 * spots, 4 * spots

    flat_basis = jnp.transpose(basis, (1, 0, 2)).reshape(rows, nvec)
    flat_images = jnp.transpose(images, (1, 0, 2)).reshape(rows, old)
    flat_hops = jnp.transpose(hops, (1, 2, 0, 3)).reshape(hops.shape[1], rows, coarse)
    half = nvec // 2
    n = half // 8
    near_order = [0] if sites > 8 else [0, 7, 8]
    far_order = [hop for hop in range(hops.shape[1]) if hop not in near_order]
    pay0, basis_here, images_here, shift, perms, near_hops = call(
        functools.partial(open_kernel, nb, spots, near_order),
        (
            shaped(nvec + chunk, nvec, BF16),
            shaped(rows, nvec, BF16),
            shaped(rows, old, BF16),
            shaped(coarse, spots * LANES, BF16),
            jax.ShapeDtypeStruct((hops.shape[1], 2 * wide, wide), BF16),
            jax.ShapeDtypeStruct((len(near_order), rows, coarse), BF16),
        ),
        stay(flat_basis),
        stay(flat_images),
        stay(neighbours),
        stay(flat_hops),
        far=(0, 1, 2, 3),
        scratch=[
            pltpu.VMEM(neighbours.shape, jnp.int32),
            pltpu.SemaphoreType.DMA((2 * PIECES + 1 + len(near_order),)),
        ],
    )
    got0 = send(pay0, core_hop, core_hop)
    kept0 = call(keep_kernel, shaped(half, nvec, F32), basis_here, images_here)

    def fetched(order):
        return call(
            functools.partial(fetch_kernel, order),
            jax.ShapeDtypeStruct((len(order), rows, coarse), BF16),
            stay(flat_hops),
            far=(0,),
            scratch=[pltpu.SemaphoreType.DMA((len(order),))],
        )

    middle = len(far_order) // 2
    far_hops = fetched(far_order[:middle])
    more_hops = fetched(far_order[middle:])
    pay1, kept1, pair = call(
        second_kernel,
        (shaped(half + 2 * chunk, nvec, BF16), shaped(half // 2, nvec, F32), shaped(2 * chunk, nvec, BF16)),
        kept0,
        got0,
        pay0,
    )
    got1 = send(pay1, x_hop, y_hop)
    far = send(pair, 0, z1_hop)
    pay2, kept2 = call(
        third_kernel,
        (shaped(half // 2 + 4 * chunk, nvec, BF16), shaped(half // 4, nvec, F32)),
        kept1,
        got1,
        pair,
        far,
    )
    got2 = send(pay2, z0_hop, x_hop)
    crossed = send(got1[half:, :], core_hop, core_hop)
    total, own = call(
        functools.partial(near_kernel, near_order),
        (shaped(rows, wide, F32), shaped(coarse, wide, BF16)),
        pair,
        got1,
        crossed,
        near_hops,
        perms,
        shift,
        scratch=[pltpu.VMEM((spots * LANES, wide), BF16)],
    )
    times = []
    if sites > 8:
        gap = 8 * spots
        times = [lax.ppermute(own, BOTH, [((d + sign * gap) % count, d) for d in range(count)]) for sign in (1, -1)]
    pay3, kept3, cross_pay = call(
        fourth_kernel,
        (shaped(half // 4, nvec, BF16), shaped(half // 8, nvec, F32), shaped(6 * chunk, nvec, BF16)),
        kept2,
        got2,
        far,
    )
    cross = send(cross_pay, core_hop, core_hop)
    got3 = send(pay3, y_hop, z1_hop)
    masked, new = call(
        functools.partial(far_kernel, nb, blk),
        (shaped(rows, wide, BF16), shaped(2 * blk, nvec, BF16)),
        own,
        got2,
        cross,
        far,
        got1,
        crossed,
        total,
        basis_here,
        far_hops,
        more_hops,
        perms,
        shift,
        *times,
        scratch=[pltpu.VMEM((3, spots * LANES, wide), BF16)],
    )
    payc = call(join_kernel, shaped(2 * n + 2 * blk, nvec, BF16), kept3, got3, new)
    turned = [pltpu.VMEM((rows, nvec), BF16), pltpu.SemaphoreType.DMA((PIECES,))]
    gotc = send(payc, z1_hop, z0_hop)
    turned_images = call(
        functools.partial(turn_kernel, nb),
        shaped(rows, nvec, BF16),
        images_here,
        masked,
        rotation,
        out_far=True,
        scratch=turned,
    )
    hop = 8 * spots
    while hop < count:
        payc = call(functools.partial(extra_kernel, n, blk), shaped(2 * n + 2 * blk, nvec, BF16), payc, gotc)
        gotc = send(payc, hop, hop)
        hop *= 2
    payc = call(functools.partial(settle_kernel, n, blk, scale), shaped(n + 2 * blk, nvec, BF16), payc, gotc)
    turned_basis = call(
        rotate_kernel, shaped(rows, nvec, BF16), basis_here, rotation, out_far=True, scratch=turned
    )
    gotc = send(payc, y_hop, z1_hop)
    payc = call(
        functools.partial(grow_kernel, n, blk, lambda core, half, y, z0, z1: pick(core, y, z1)),
        shaped(2 * n + 2 * blk, nvec, BF16),
        payc,
        gotc,
    )
    n *= 2
    got_ab = send(payc, z0_hop + x_hop, x_hop + y_hop)
    got_b = send(payc, x_hop, y_hop)
    got_a = send(payc, z0_hop, x_hop)
    payc = call(
        functools.partial(
            join_four_kernel,
            n,
            blk,
            lambda core, half, y, z0, z1: pick(core, z0, half),
            lambda core, half, y, z0, z1: pick(core, half, y),
        ),
        shaped(4 * n + 2 * blk, nvec, BF16),
        payc,
        got_a,
        got_b,
        got_ab,
    )
    n *= 4
    gotc = send(payc, core_hop, core_hop)
    projected = call(
        functools.partial(final_kernel, n, blk, scale),
        shaped(nvec, nvec, F32),
        payc,
        gotc,
        out_far=True,
        scratch=[pltpu.VMEM((nvec, nvec), F32), pltpu.SemaphoreType.DMA((4,))],
    )

    def back(x):
        return jnp.transpose(x.reshape(modes_here, nb, nvec), (1, 0, 2))

    return projected, back(turned_basis), back(turned_images)


def solution(mesh):
    placed = (
        P("site", "mode", None),
        P("site", "mode", None),
        P("site", None, "mode", None),
        P("site", None),
        P(),
    )
    return jax.shard_map(
        program,
        mesh=mesh,
        in_specs=placed,
        out_specs=(P(), P("site", "mode", None), P("site", "mode", None)),
        check_vma=False,
    )
```

```python
import functools
import math

import jax
import jax.numpy as jnp
from jax import lax
from jax.experimental import pallas as pl
from jax.experimental.pallas import tpu as pltpu
from jax.sharding import PartitionSpec as P


F32 = jnp.float32
BF16 = jnp.bfloat16
BOTH = ("site", "mode")
LANES = 128
PIECES = 2


def dot_nn(a, b):
    return lax.dot_general(a, b, (((1,), (0,)), ((), ())), preferred_element_type=F32)


def dot_tn(a, b):
    return lax.dot_general(a, b, (((0,), (0,)), ((), ())), preferred_element_type=F32)


def onehot(shape, test):
    rows = lax.broadcasted_iota(jnp.int32, shape, 0)
    cols = lax.broadcasted_iota(jnp.int32, shape, 1)
    return jnp.where(test(rows, cols), 1.0, 0.0).astype(BF16)


def split(x):
    high = x.astype(BF16)
    low = (x - high.astype(F32)).astype(BF16)
    return high, low


def place():
    mode = lax.axis_index("mode")
    site = lax.axis_index("site")
    core = lax.rem(mode, 2)
    half = lax.div(mode, 2)
    y = lax.rem(site, 2)
    z0 = lax.rem(lax.div(site, 2), 2)
    z1 = lax.rem(lax.div(site, 4), 2)
    return core, half, y, z0, z1


def pick(core, first, second):
    return first * (1 - core) + second * core


def rows_at(index, count):
    return pl.ds(pl.multiple_of(index * count, count), count)


def call(kernel, outs, *args, scratch=(), flops=10**8, moved=2 * 10**6, smem=(), far=(), out_far=False, alias={}):
    vmem = pl.BlockSpec(memory_space=pltpu.VMEM)
    scalars = pl.BlockSpec(memory_space=pltpu.SMEM)
    distant = pl.BlockSpec(memory_space=pltpu.HBM)
    return pl.pallas_call(
        kernel,
        out_shape=outs,
        in_specs=[scalars if i in smem else distant if i in far else vmem for i in range(len(args))],
        out_specs=jax.tree.map(lambda _: pl.BlockSpec(memory_space=pl.ANY) if out_far else vmem, outs),
        scratch_shapes=scratch,
        input_output_aliases=alias,
        compiler_params=pltpu.CompilerParams(vmem_limit_bytes=16 * 2**20),
        cost_estimate=pl.CostEstimate(flops=flops, bytes_accessed=moved, transcendentals=0),
    )(*args)


def stay(x):
    return pltpu.with_memory_space_constraint(x, pltpu.HBM)


def shaped(rows, cols, dtype):
    return jax.ShapeDtypeStruct((rows, cols), dtype)


def open_kernel(nb, spots, near, basis_far, images_far, table_far, pay, basis, images, shift, perms, table, sems):
    rows, nvec = basis.shape
    old = images.shape[1]
    blk = nvec - old
    step = rows // PIECES
    copies = []
    for j, (far, here) in enumerate(((basis_far, basis), (images_far, images))):
        for i in range(PIECES):
            span = pl.ds(i * step, step)
            copies.append(pltpu.make_async_copy(far.at[span], here.at[span], sems.at[j * PIECES + i]))
    small = pltpu.make_async_copy(table_far, table, sems.at[2 * PIECES])
    small.start()
    for copy in copies:
        copy.start()
    core = place()[0]
    top = nvec // 2
    wide = nb * blk
    share = 2 * shift.shape[0] // spots
    shift[...] = onehot(
        shift.shape,
        lambda r, c: (lax.rem(c, LANES) < share) & (lax.div(c, LANES) * share + lax.rem(c, LANES) == r),
    )
    gather = onehot((LANES, rows), lambda r, c: lax.div(c, nb) == r)
    spread = onehot((LANES, wide), lambda r, c: r - (LANES - blk) == lax.rem(c, blk))
    small.wait()
    choose(near, nb, blk, table[...], perms)
    for copy in copies[:PIECES]:
        copy.wait()
    tiled = dot_nn(basis[:, nvec - LANES :], spread)
    row = lax.broadcasted_iota(jnp.int32, (rows, wide), 0)
    col = lax.broadcasted_iota(jnp.int32, (rows, wide), 1)
    tiled = jnp.where(lax.rem(row, nb) == lax.div(col, blk), tiled, 0.0).astype(BF16)
    merged = dot_nn(gather, tiled).astype(BF16)
    groups = nvec // LANES
    each = LANES // groups
    for g in range(groups):
        pay[2 * top :, g * LANES : (g + 1) * LANES] = merged[g * each : (g + 1) * each]
    give = pl.ds(pl.multiple_of((1 - core) * top, top), top)
    part = None
    for i in range(PIECES):
        span = pl.ds(i * step, step)
        copies[PIECES + i].wait()
        piece = dot_tn(basis[span, give], images[span, :])
        part = piece if part is None else part + piece
    high, low = split(part)
    pay[:top, :old] = high
    pay[:top, old:] = jnp.zeros((top, blk), BF16)
    pay[top : 2 * top, :old] = low
    pay[top : 2 * top, old:] = jnp.zeros((top, blk), BF16)


def fetch_kernel(order, far, near, sems):
    copies = [pltpu.make_async_copy(far.at[hop], near.at[i], sems.at[i]) for i, hop in enumerate(order)]
    for copy in copies:
        copy.start()
    for copy in copies:
        copy.wait()


def keep_kernel(basis, images, kept):
    nvec = basis.shape[1]
    old = images.shape[1]
    core = place()[0]
    top = nvec // 2
    mine = basis[:, pl.ds(pl.multiple_of(core * top, top), top)]
    kept[:, :old] = dot_tn(mine, images[...])
    kept[:, old:] = jnp.zeros((top, nvec - old), F32)


def put(far, held, sems, pieces, work):
    step = held.shape[0] // pieces
    copies = []
    for i in range(pieces):
        span = pl.ds(i * step, step)
        held[span, :] = work(span)
        copy = pltpu.make_async_copy(held.at[span], far.at[span], sems.at[i])
        copy.start()
        copies.append(copy)
    for copy in copies:
        copy.wait()


def rotate_kernel(basis, rotation, far, held, sems):
    put(far, held, sems, PIECES, lambda span: dot_nn(basis[span, :], rotation[...]).astype(BF16))


def joined(kept, got, start, count):
    whole = kept.shape[0]
    rows = pl.ds(pl.multiple_of(start, count), count)
    lows = pl.ds(pl.multiple_of(start + whole, count), count)
    return kept[rows, :] + (got[rows, :].astype(F32) + got[lows, :].astype(F32))


def second_kernel(kept, got, pay, out, rest, pair):
    core, half, y, _, _ = place()
    whole = kept.shape[0]
    n = whole // 2
    bit = pick(core, half, y)
    out[:n, :], out[n : 2 * n, :] = split(joined(kept, got, (1 - bit) * n, n))
    rest[...] = joined(kept, got, bit * n, n)
    each = got.shape[0] - 2 * whole
    pair[rows_at(core, each), :] = pay[2 * whole :, :]
    pair[rows_at(1 - core, each), :] = got[2 * whole :, :]
    out[2 * n :, :] = pair[...]


def third_kernel(kept, got, pair, far, out, rest):
    core, half, _, z0, _ = place()
    whole = kept.shape[0]
    n = whole // 2
    bit = pick(core, z0, half)
    out[:n, :], out[n : 2 * n, :] = split(joined(kept, got, (1 - bit) * n, n))
    rest[...] = joined(kept, got, bit * n, n)
    each = pair.shape[0]
    at = pick(core, 1 - half, 0)
    out[pl.ds(pl.multiple_of(2 * n + at * each, each), each), :] = got[2 * whole :, :]
    out[pl.ds(pl.multiple_of(2 * n + (1 - at) * each, each), each), :] = jnp.where(
        core == 0, pair[...], far[...]
    )


def fourth_kernel(kept, got, far, out, rest, cross):
    core, _, y, _, z1 = place()
    whole = kept.shape[0]
    n = whole // 2
    bit = pick(core, y, z1)
    out[:n, :], out[n:, :] = split(joined(kept, got, (1 - bit) * n, n))
    rest[...] = joined(kept, got, bit * n, n)
    area = got.shape[0] - 2 * whole
    cross[:area, :] = got[2 * whole :, :]
    cross[area:, :] = far[...]


def choose(near, nb, blk, table, perms):
    hops = perms.shape[0]
    wide = nb * blk
    row = lax.broadcasted_iota(jnp.int32, (2 * wide, wide), 0)
    col = lax.broadcasted_iota(jnp.int32, (hops - 1, wide), 1)
    repeat = onehot((nb, wide), lambda r, c: lax.div(c, blk) == r)
    entry = dot_tn(table.astype(F32).astype(BF16), repeat).astype(jnp.int32)
    piece = lax.div(entry, nb)
    wanted = (entry - piece * nb) * blk + lax.rem(col, blk)
    aside = wanted + jnp.where(piece > 0, wide, 0)
    perms[0] = onehot((2 * wide, wide), lambda r, c: r == c)
    for hop in range(1, hops):
        target = (wanted if hop in near else aside)[hop - 1 : hop, :]
        perms[hop] = jnp.where(row == target, 1.0, 0.0).astype(BF16)


def half_site(shift, piece):
    rows, nvec = piece.shape
    groups = nvec // LANES
    each = LANES // groups
    chunks = rows // each
    parts = [
        piece[m * each : (m + 1) * each, g * LANES : (g + 1) * LANES] for m in range(chunks) for g in range(groups)
    ]
    return dot_nn(shift, jnp.concatenate(parts, axis=0))


def ordered(half, first, second):
    low = jnp.where(half == 0, first, second)
    high = jnp.where(half == 0, second, first)
    return jnp.concatenate([low, high], axis=0).astype(BF16)


def near_kernel(order, spots_of, pair, got, crossed, hops, more, perms, shift, total, own_out):
    core, half, _, _, _ = place()
    each = pair.shape[0]
    wide = own_out.shape[1]
    area = got.shape[0]
    apart = jnp.where(core == 0, got[area - each :, :], crossed[...])
    own = ordered(half, half_site(shift[...], pair[...]), half_site(shift[...], apart))
    own_out[...] = own
    rows = total.shape[0]
    mixed = [dot_nn(own, perms[hop, :wide, :]).astype(BF16) for hop in order]
    step = rows // 2
    for r in range(2):
        span = pl.ds(r * step, step)
        part = None
        for i, hop in enumerate(order):
            group, at = spots_of[hop]
            piece = dot_nn((hops, more)[group][at, span, :], mixed[i])
            part = piece if part is None else part + piece
        total[span, :] = part


def far_kernel(nb, blk, spots_of, own, got2, cross, far, got1, crossed, total, basis, hops, more, perms, shift, *refs):
    times, (masked, new_out) = refs[:-2], refs[-2:]
    core, half, _, _, _ = place()
    each = far.shape[0]
    wide = own.shape[1]
    rows = basis.shape[0]
    nvec = basis.shape[1]
    first = core == 0
    mine = got2[got2.shape[0] - 2 * each :, :]
    theirs = cross[: 2 * each, :]
    sites = []
    one = jnp.where(first, theirs, mine)
    two = jnp.where(first, mine, theirs)
    move = shift[...]
    near_site = ordered(
        half,
        half_site(move, jnp.where(first, crossed[...], got1[got1.shape[0] - each :, :])),
        half_site(move, one[:each]),
    )
    long_site = ordered(
        half,
        half_site(move, jnp.where(first, cross[2 * each :, :], far[...])),
        half_site(move, one[each:]),
    )
    mid_site = ordered(0, half_site(move, two[:each]), half_site(move, two[each:]))
    sites = {1: long_site, 4: long_site, 2: mid_site, 5: mid_site, 3: near_site, 6: near_site}
    for k, ref in enumerate(times):
        sites[7 + k] = ref[...]
    order = sorted(sites)
    mixed = [
        dot_nn(jnp.concatenate([own[...], sites[hop]], axis=1), perms[hop]).astype(BF16) for hop in order
    ]
    step = rows // 2
    sums = jnp.zeros((wide, nvec), F32)
    for r in range(2):
        span = pl.ds(r * step, step)
        part = total[span, :]
        for i, hop in enumerate(order):
            group, at = spots_of[hop]
            part = part + dot_nn((None, hops, more)[group][at, span, :], mixed[i])
        row = lax.broadcasted_iota(jnp.int32, (step, wide), 0)
        col = lax.broadcasted_iota(jnp.int32, (step, wide), 1)
        chosen = jnp.where(lax.rem(row, nb) == lax.div(col, blk), part, 0.0).astype(BF16)
        masked[span, :] = chosen
        sums = sums + dot_tn(chosen, basis[span, :])
    new = sums[:blk]
    for b in range(1, nb):
        new = new + sums[b * blk : (b + 1) * blk]
    new_out[:blk, :], new_out[blk:, :] = split(new)


def join_kernel(kept, got, new, out):
    n = kept.shape[0]
    total = kept[...] + (got[:n, :].astype(F32) + got[n:, :].astype(F32))
    out[:n, :], out[n : 2 * n, :] = split(total)
    out[2 * n :, :] = new[...]


def turn_kernel(nb, images, masked, rotation, far, held, sems):
    old = images.shape[1]
    tail = rotation[old:, :]
    deep = jnp.concatenate([tail] * nb, axis=0)
    put(
        far,
        held,
        sems,
        PIECES,
        lambda span: (dot_nn(images[span, :], rotation[:old, :]) + dot_nn(masked[span, :], deep)).astype(BF16),
    )


def value(ref, start, count):
    return ref[start : start + count, :].astype(F32) + ref[start + count : start + 2 * count, :].astype(F32)


def extra_kernel(n, blk, pay, got, out):
    out[:n, :], out[n : 2 * n, :] = split(value(pay, 0, n) + value(got, 0, n))
    out[2 * n : 2 * n + blk, :], out[2 * n + blk :, :] = split(value(pay, 2 * n, blk) + value(got, 2 * n, blk))


def settle_kernel(n, blk, scale, pay, got, out):
    out[:n, :] = ((value(pay, 0, n) + value(got, 0, n)) * scale).astype(BF16)
    out[n : n + blk, :], out[n + blk :, :] = split(value(pay, 2 * n, blk) + value(got, 2 * n, blk))


def grow_kernel(n, blk, chooser, pay, got, out):
    bit = chooser(*place())
    out[rows_at(bit, n), :] = pay[:n, :]
    out[rows_at(1 - bit, n), :] = got[:n, :]
    out[2 * n : 2 * n + blk, :], out[2 * n + blk :, :] = split(value(pay, n, blk) + value(got, n, blk))


def join_four_kernel(n, blk, first, second, pay, got_a, got_b, got_ab, out):
    spot = place()
    a, b = first(*spot), second(*spot)
    out[rows_at(2 * b + a, n), :] = pay[:n, :]
    out[rows_at(2 * b + 1 - a, n), :] = got_a[:n, :]
    out[rows_at(2 * (1 - b) + a, n), :] = got_b[:n, :]
    out[rows_at(2 * (1 - b) + 1 - a, n), :] = got_ab[:n, :]
    new = (value(pay, n, blk) + value(got_a, n, blk)) + (value(got_b, n, blk) + value(got_ab, n, blk))
    out[4 * n : 4 * n + blk, :], out[4 * n + blk :, :] = split(new)


def early_kernel(n, pay, far, held, sem):
    core = place()[0]
    width = held.shape[1]
    held[...] = pay[:n, :width].astype(F32)
    copy = pltpu.make_async_copy(held, far.at[rows_at(core, n), :width], sem)
    copy.start()
    copy.wait()


def final_kernel(n, blk, scale, pay, got, begun, far, held, edge, sems):
    nvec = far.shape[1]
    core = place()[0]
    width = nvec - LANES
    new = (value(pay, n, blk) + value(got, n, blk)) * scale
    tall = jnp.concatenate([jnp.zeros((LANES - blk, nvec), F32), new], axis=0)
    step = n // 2
    copies = []
    for i in range(2):
        held[i * step : (i + 1) * step, :width] = got[i * step : (i + 1) * step, :width].astype(F32)
        span = pl.ds(pl.multiple_of((1 - core) * n + i * step, step), step)
        copies.append(pltpu.make_async_copy(held.at[pl.ds(i * step, step)], far.at[span, :width], sems.at[i]))
        copies[-1].start()
    lane = lax.broadcasted_iota(jnp.int32, (n, LANES), 1)
    edge[...] = tall.T
    for source, side in ((pay, core), (got, 1 - core)):
        span = rows_at(side, n)
        edge[span, :] = jnp.where(lane < LANES - blk, source[:n, width:].astype(F32), edge[span, :])
    copies.append(pltpu.make_async_copy(edge, far.at[:, width:], sems.at[2]))
    copies[-1].start()
    for copy in copies:
        copy.wait()


def program(basis, images, hops, neighbours, rotation):
    nb, modes_here, nvec = basis.shape
    old = images.shape[2]
    blk = nvec - old
    sites = lax.axis_size("site")
    spots = lax.axis_size("mode")
    count = sites * spots
    rows = nb * modes_here
    coarse = hops.shape[3]
    wide = nb * blk
    chunk = wide * LANES // nvec
    scale = 1.0 / math.sqrt(count * rows)

    def send(x, first, second):
        pairs = [(d, d ^ hop) for d in range(count) for hop in [second if d % 2 else first] if hop]
        return lax.ppermute(x, BOTH, pairs)

    core_hop, x_hop, y_hop, z0_hop, z1_hop = 1, 2, spots, 2 * spots, 4 * spots

    flat_basis = jnp.transpose(basis, (1, 0, 2)).reshape(rows, nvec)
    flat_images = jnp.transpose(images, (1, 0, 2)).reshape(rows, old)
    flat_hops = jnp.transpose(hops, (1, 2, 0, 3)).reshape(hops.shape[1], rows, coarse)
    half = nvec // 2
    n = half // 8
    near_order = [0] if sites > 8 else [0, 7, 8]
    far_order = [hop for hop in range(hops.shape[1]) if hop not in near_order]
    pay0, basis_here, images_here, shift, perms = call(
        functools.partial(open_kernel, nb, spots, near_order),
        (
            shaped(nvec + chunk, nvec, BF16),
            shaped(rows, nvec, BF16),
            shaped(rows, old, BF16),
            shaped(coarse // 2, spots * LANES // 2, BF16),
            jax.ShapeDtypeStruct((hops.shape[1], 2 * wide, wide), BF16),
        ),
        stay(flat_basis),
        stay(flat_images),
        stay(neighbours),
        far=(0, 1, 2),
        scratch=[
            pltpu.VMEM(neighbours.shape, jnp.int32),
            pltpu.SemaphoreType.DMA((2 * PIECES + 1,)),
        ],
    )

    def fetched(order):
        return call(
            functools.partial(fetch_kernel, order),
            jax.ShapeDtypeStruct((len(order), rows, coarse), BF16),
            stay(flat_hops),
            far=(0,),
            scratch=[pltpu.SemaphoreType.DMA((len(order),))],
        )

    got0 = send(pay0, core_hop, core_hop)
    middle = len(far_order) // 2
    groups = (near_order[:2], near_order[2:] + far_order[:middle], far_order[middle:])
    spots_of = {hop: (g, i) for g, group in enumerate(groups) for i, hop in enumerate(group)}
    near_hops = fetched(groups[0])
    kept0 = call(keep_kernel, shaped(half, nvec, F32), basis_here, images_here)
    far_hops = fetched(groups[1])
    more_hops = fetched(groups[2])
    pay1, kept1, pair = call(
        second_kernel,
        (shaped(half + 2 * chunk, nvec, BF16), shaped(half // 2, nvec, F32), shaped(2 * chunk, nvec, BF16)),
        kept0,
        got0,
        pay0,
    )
    got1 = send(pay1, x_hop, y_hop)
    far = send(pair, 0, z1_hop)
    pay2, kept2 = call(
        third_kernel,
        (shaped(half // 2 + 4 * chunk, nvec, BF16), shaped(half // 4, nvec, F32)),
        kept1,
        got1,
        pair,
        far,
    )
    got2 = send(pay2, z0_hop, x_hop)
    crossed = send(got1[half:, :], core_hop, core_hop)
    total, own = call(
        functools.partial(near_kernel, near_order, spots_of),
        (shaped(rows, wide, F32), shaped(coarse, wide, BF16)),
        pair,
        got1,
        crossed,
        near_hops,
        far_hops,
        perms,
        shift,
    )
    times = []
    if sites > 8:
        gap = 8 * spots
        times = [lax.ppermute(own, BOTH, [((d + sign * gap) % count, d) for d in range(count)]) for sign in (1, -1)]
    pay3, kept3, cross_pay = call(
        fourth_kernel,
        (shaped(half // 4, nvec, BF16), shaped(half // 8, nvec, F32), shaped(6 * chunk, nvec, BF16)),
        kept2,
        got2,
        far,
    )
    cross = send(cross_pay, core_hop, core_hop)
    got3 = send(pay3, y_hop, z1_hop)
    masked, new = call(
        functools.partial(far_kernel, nb, blk, spots_of),
        (shaped(rows, wide, BF16), shaped(2 * blk, nvec, BF16)),
        own,
        got2,
        cross,
        far,
        got1,
        crossed,
        total,
        basis_here,
        far_hops,
        more_hops,
        perms,
        shift,
        *times,
    )
    payc = call(join_kernel, shaped(2 * n + 2 * blk, nvec, BF16), kept3, got3, new)
    turned = [pltpu.VMEM((rows, nvec), BF16), pltpu.SemaphoreType.DMA((PIECES,))]
    gotc = send(payc, z1_hop, z0_hop)
    turned_images = call(
        functools.partial(turn_kernel, nb),
        shaped(rows, nvec, BF16),
        images_here,
        masked,
        rotation,
        out_far=True,
        scratch=turned,
    )
    hop = 8 * spots
    while hop < count:
        payc = call(functools.partial(extra_kernel, n, blk), shaped(2 * n + 2 * blk, nvec, BF16), payc, gotc)
        gotc = send(payc, hop, hop)
        hop *= 2
    payc = call(functools.partial(settle_kernel, n, blk, scale), shaped(n + 2 * blk, nvec, BF16), payc, gotc)
    turned_basis = call(
        rotate_kernel, shaped(rows, nvec, BF16), basis_here, rotation, out_far=True, scratch=turned
    )
    gotc = send(payc, y_hop, z1_hop)
    payc = call(
        functools.partial(grow_kernel, n, blk, lambda core, half, y, z0, z1: pick(core, y, z1)),
        shaped(2 * n + 2 * blk, nvec, BF16),
        payc,
        gotc,
    )
    n *= 2
    got_ab = send(payc, z0_hop + x_hop, x_hop + y_hop)
    got_b = send(payc, x_hop, y_hop)
    got_a = send(payc, z0_hop, x_hop)
    payc = call(
        functools.partial(
            join_four_kernel,
            n,
            blk,
            lambda core, half, y, z0, z1: pick(core, z0, half),
            lambda core, half, y, z0, z1: pick(core, half, y),
        ),
        shaped(4 * n + 2 * blk, nvec, BF16),
        payc,
        got_a,
        got_b,
        got_ab,
    )
    n *= 4
    gotc = send(payc, core_hop, core_hop)
    begun = call(
        functools.partial(early_kernel, n),
        shaped(nvec, nvec, F32),
        payc,
        out_far=True,
        scratch=[pltpu.VMEM((n, nvec - LANES), F32), pltpu.SemaphoreType.DMA],
    )
    projected = call(
        functools.partial(final_kernel, n, blk, scale),
        shaped(nvec, nvec, F32),
        payc,
        gotc,
        begun,
        far=(2,),
        out_far=True,
        alias={2: 0},
        scratch=[
            pltpu.VMEM((n, nvec - LANES), F32),
            pltpu.VMEM((nvec, LANES), F32),
            pltpu.SemaphoreType.DMA((3,)),
        ],
    )

    def back(x):
        return jnp.transpose(x.reshape(modes_here, nb, nvec), (1, 0, 2))

    return projected, back(turned_basis), back(turned_images)


def solution(mesh):
    placed = (
        P("site", "mode", None),
        P("site", "mode", None),
        P("site", None, "mode", None),
        P("site", None),
        P(),
    )
    return jax.shard_map(
        program,
        mesh=mesh,
        in_specs=placed,
        out_specs=(P(), P("site", "mode", None), P("site", "mode", None)),
        check_vma=False,
    )
```

```python
import functools
import math

import jax
import jax.numpy as jnp
from jax import lax
from jax.experimental import pallas as pl
from jax.experimental.pallas import tpu as pltpu
from jax.sharding import PartitionSpec as P


F32 = jnp.float32
BF16 = jnp.bfloat16
BOTH = ("site", "mode")
LANES = 128
PIECES = 2


def dot_nn(a, b):
    return lax.dot_general(a, b, (((1,), (0,)), ((), ())), preferred_element_type=F32)


def dot_tn(a, b):
    return lax.dot_general(a, b, (((0,), (0,)), ((), ())), preferred_element_type=F32)


def onehot(shape, test):
    rows = lax.broadcasted_iota(jnp.int32, shape, 0)
    cols = lax.broadcasted_iota(jnp.int32, shape, 1)
    return jnp.where(test(rows, cols), 1.0, 0.0).astype(BF16)


def split(x):
    high = x.astype(BF16)
    low = (x - high.astype(F32)).astype(BF16)
    return high, low


def place():
    mode = lax.axis_index("mode")
    site = lax.axis_index("site")
    core = lax.rem(mode, 2)
    half = lax.div(mode, 2)
    y = lax.rem(site, 2)
    z0 = lax.rem(lax.div(site, 2), 2)
    z1 = lax.rem(lax.div(site, 4), 2)
    return core, half, y, z0, z1


def pick(core, first, second):
    return first * (1 - core) + second * core


def rows_at(index, count):
    return pl.ds(pl.multiple_of(index * count, count), count)


def call(kernel, outs, *args, scratch=(), flops=10**8, moved=2 * 10**6, smem=(), far=(), out_far=False, alias={}):
    vmem = pl.BlockSpec(memory_space=pltpu.VMEM)
    scalars = pl.BlockSpec(memory_space=pltpu.SMEM)
    distant = pl.BlockSpec(memory_space=pltpu.HBM)
    return pl.pallas_call(
        kernel,
        out_shape=outs,
        in_specs=[scalars if i in smem else distant if i in far else vmem for i in range(len(args))],
        out_specs=jax.tree.map(lambda _: pl.BlockSpec(memory_space=pl.ANY) if out_far else vmem, outs),
        scratch_shapes=scratch,
        input_output_aliases=alias,
        compiler_params=pltpu.CompilerParams(vmem_limit_bytes=16 * 2**20),
        cost_estimate=pl.CostEstimate(flops=flops, bytes_accessed=moved, transcendentals=0),
    )(*args)


def stay(x):
    return pltpu.with_memory_space_constraint(x, pltpu.HBM)


def shaped(rows, cols, dtype):
    return jax.ShapeDtypeStruct((rows, cols), dtype)


def open_kernel(nb, spots, near, basis_far, images_far, table_far, pay, basis, images, shift, perms, table, sems):
    rows, nvec = basis.shape
    old = images.shape[1]
    blk = nvec - old
    step = rows // PIECES
    copies = []
    for j, (far, here) in enumerate(((basis_far, basis), (images_far, images))):
        for i in range(PIECES):
            span = pl.ds(i * step, step)
            copies.append(pltpu.make_async_copy(far.at[span], here.at[span], sems.at[j * PIECES + i]))
    small = pltpu.make_async_copy(table_far, table, sems.at[2 * PIECES])
    small.start()
    for copy in copies:
        copy.start()
    core = place()[0]
    top = nvec // 2
    wide = nb * blk
    share = 2 * shift.shape[0] // spots
    shift[...] = onehot(
        shift.shape,
        lambda r, c: (lax.rem(c, LANES) < share) & (lax.div(c, LANES) * share + lax.rem(c, LANES) == r),
    )
    gather = onehot((LANES, rows), lambda r, c: lax.div(c, nb) == r)
    spread = onehot((LANES, wide), lambda r, c: r - (LANES - blk) == lax.rem(c, blk))
    small.wait()
    choose(near, nb, blk, table[...], perms)
    for copy in copies[:PIECES]:
        copy.wait()
    tiled = dot_nn(basis[:, nvec - LANES :], spread)
    row = lax.broadcasted_iota(jnp.int32, (rows, wide), 0)
    col = lax.broadcasted_iota(jnp.int32, (rows, wide), 1)
    tiled = jnp.where(lax.rem(row, nb) == lax.div(col, blk), tiled, 0.0).astype(BF16)
    merged = dot_nn(gather, tiled).astype(BF16)
    groups = nvec // LANES
    each = LANES // groups
    for g in range(groups):
        pay[2 * top :, g * LANES : (g + 1) * LANES] = merged[g * each : (g + 1) * each]
    give = pl.ds(pl.multiple_of((1 - core) * top, top), top)
    part = None
    for i in range(PIECES):
        span = pl.ds(i * step, step)
        copies[PIECES + i].wait()
        piece = dot_tn(basis[span, give], images[span, :])
        part = piece if part is None else part + piece
    high, low = split(part)
    pay[:top, :old] = high
    pay[:top, old:] = jnp.zeros((top, blk), BF16)
    pay[top : 2 * top, :old] = low
    pay[top : 2 * top, old:] = jnp.zeros((top, blk), BF16)


def fetch_kernel(order, far, near, sems):
    copies = [pltpu.make_async_copy(far.at[hop], near.at[i], sems.at[i]) for i, hop in enumerate(order)]
    for copy in copies:
        copy.start()
    for copy in copies:
        copy.wait()


def keep_kernel(basis, images, kept):
    nvec = basis.shape[1]
    old = images.shape[1]
    core = place()[0]
    top = nvec // 2
    mine = basis[:, pl.ds(pl.multiple_of(core * top, top), top)]
    kept[:, :old] = dot_tn(mine, images[...])
    kept[:, old:] = jnp.zeros((top, nvec - old), F32)


def put(far, held, sems, pieces, work):
    step = held.shape[0] // pieces
    copies = []
    for i in range(pieces):
        span = pl.ds(i * step, step)
        held[span, :] = work(span)
        copy = pltpu.make_async_copy(held.at[span], far.at[span], sems.at[i])
        copy.start()
        copies.append(copy)
    for copy in copies:
        copy.wait()


def rotate_kernel(basis, rotation, far, held, sems):
    put(far, held, sems, PIECES, lambda span: dot_nn(basis[span, :], rotation[...]).astype(BF16))


def joined(kept, got, start, count):
    whole = kept.shape[0]
    rows = pl.ds(pl.multiple_of(start, count), count)
    lows = pl.ds(pl.multiple_of(start + whole, count), count)
    return kept[rows, :] + (got[rows, :].astype(F32) + got[lows, :].astype(F32))


def second_kernel(kept, got, pay, out, rest, pair):
    core, half, y, _, _ = place()
    whole = kept.shape[0]
    n = whole // 2
    bit = pick(core, half, y)
    out[:n, :], out[n : 2 * n, :] = split(joined(kept, got, (1 - bit) * n, n))
    rest[...] = joined(kept, got, bit * n, n)
    each = got.shape[0] - 2 * whole
    pair[rows_at(core, each), :] = pay[2 * whole :, :]
    pair[rows_at(1 - core, each), :] = got[2 * whole :, :]
    out[2 * n :, :] = pair[...]


def third_kernel(kept, got, pair, far, out, side_out, both_out, rest):
    core, half, y, z0, z1 = place()
    whole = kept.shape[0]
    n = whole // 4
    b, a = pick(core, z0, half), pick(core, y, z1)
    for target, spot in ((out, 2 * (1 - b) + a), (side_out, 2 * b + 1 - a), (both_out, 2 * (1 - b) + 1 - a)):
        target[:n, :], target[n : 2 * n, :] = split(joined(kept, got, spot * n, n))
    rest[...] = joined(kept, got, (2 * b + a) * n, n)
    each = pair.shape[0]
    at = pick(core, 1 - half, 0)
    out[pl.ds(pl.multiple_of(2 * n + at * each, each), each), :] = got[2 * whole :, :]
    out[pl.ds(pl.multiple_of(2 * n + (1 - at) * each, each), each), :] = jnp.where(
        core == 0, pair[...], far[...]
    )


def fourth_kernel(got, far, cross):
    area = cross.shape[0] - far.shape[0]
    cross[:area, :] = got[got.shape[0] - area :, :]
    cross[area:, :] = far[...]


def choose(near, nb, blk, table, perms):
    hops = perms.shape[0]
    wide = nb * blk
    row = lax.broadcasted_iota(jnp.int32, (2 * wide, wide), 0)
    col = lax.broadcasted_iota(jnp.int32, (hops - 1, wide), 1)
    repeat = onehot((nb, wide), lambda r, c: lax.div(c, blk) == r)
    entry = dot_tn(table.astype(F32).astype(BF16), repeat).astype(jnp.int32)
    piece = lax.div(entry, nb)
    wanted = (entry - piece * nb) * blk + lax.rem(col, blk)
    aside = wanted + jnp.where(piece > 0, wide, 0)
    perms[0] = onehot((2 * wide, wide), lambda r, c: r == c)
    for hop in range(1, hops):
        target = (wanted if hop in near else aside)[hop - 1 : hop, :]
        perms[hop] = jnp.where(row == target, 1.0, 0.0).astype(BF16)


def half_site(shift, piece):
    rows, nvec = piece.shape
    groups = nvec // LANES
    each = LANES // groups
    chunks = rows // each
    parts = [
        piece[m * each : (m + 1) * each, g * LANES : (g + 1) * LANES] for m in range(chunks) for g in range(groups)
    ]
    return dot_nn(shift, jnp.concatenate(parts, axis=0))


def ordered(half, first, second):
    low = jnp.where(half == 0, first, second)
    high = jnp.where(half == 0, second, first)
    return jnp.concatenate([low, high], axis=0).astype(BF16)


def pulled(order, far, near, sems):
    copies = [pltpu.make_async_copy(far.at[hop], near.at[i], sems.at[i]) for i, hop in enumerate(order)]
    for copy in copies:
        copy.start()
    return copies


def near_kernel(here, later, pair, got, crossed, hops, more, perms, shift, total, own_out):
    core, half, _, _, _ = place()
    each = pair.shape[0]
    wide = own_out.shape[1]
    area = got.shape[0]
    apart = jnp.where(core == 0, got[area - each :, :], crossed[...])
    own = ordered(half, half_site(shift[...], pair[...]), half_site(shift[...], apart))
    own_out[...] = own
    rows = total.shape[0]
    terms = [(hops, i, hop) for i, hop in enumerate(here)]
    terms += [(more, more.shape[0] - len(later) + i, hop) for i, hop in enumerate(later)]
    mixed = [dot_nn(own, perms[hop, :wide, :]).astype(BF16) for _, _, hop in terms]
    step = rows // 2
    for r in range(2):
        span = pl.ds(r * step, step)
        part = None
        for (source, at, _), term in zip(terms, mixed):
            piece = dot_nn(source[at, span, :], term)
            part = piece if part is None else part + piece
        total[span, :] = part


def mixture(perms, own, site, hop):
    return dot_nn(jnp.concatenate([own[...], site], axis=1), perms[hop]).astype(BF16)


def middle_kernel(ahead, own, got2, got1, total, hops, hops_far, perms, shift, out, next_hops, sems):
    copies = pulled(ahead, hops_far, next_hops, sems)
    core, half, _, _, _ = place()
    first = core == 0
    each = 2 * LANES * LANES // got2.shape[1]
    mine = got2[got2.shape[0] - 2 * each :, :]
    move = shift[...]
    site = ordered(
        pick(core, 0, half),
        half_site(move, jnp.where(first, mine[:each], got1[got1.shape[0] - each :, :])),
        half_site(move, jnp.where(first, mine[each:], mine[:each])),
    )
    mixed = [mixture(perms, own, site, 2 + core + 3 * i) for i in range(2)]
    step = out.shape[0] // 2
    for r in range(2):
        span = pl.ds(r * step, step)
        part = total[span, :]
        for i in range(2):
            part = part + dot_nn(hops[2 * core + i, span, :], mixed[i])
        out[span, :] = part
    for copy in copies:
        copy.wait()


def far_kernel(nb, blk, order, own, got2, cross, far, crossed, total, basis, hops, more, perms, shift, *refs):
    times, (masked, new_out) = refs[:-2], refs[-2:]
    core, half, _, _, _ = place()
    each = far.shape[0]
    wide = own.shape[1]
    rows = basis.shape[0]
    nvec = basis.shape[1]
    first = core == 0
    mine = got2[got2.shape[0] - 2 * each :, :]
    theirs = cross[: 2 * each, :]
    move = shift[...]
    site = ordered(
        pick(core, half, 0),
        half_site(move, jnp.where(first, crossed[...], theirs[:each])),
        half_site(move, jnp.where(first, theirs[:each], theirs[each:])),
    )
    long_site = ordered(
        half,
        half_site(move, jnp.where(first, cross[2 * each :, :], far[...])),
        half_site(move, jnp.where(first, theirs[each:], mine[each:])),
    )
    terms = [(more, 2 * (1 - core) + i, mixture(perms, own, site, 3 - core + 3 * i)) for i in range(2)]
    for i, hop in enumerate(order):
        term = long_site if hop in (1, 4) else times[hop - 7][...]
        terms.append((hops, i, mixture(perms, own, term, hop)))
    step = rows // 2
    sums = jnp.zeros((wide, nvec), F32)
    for r in range(2):
        span = pl.ds(r * step, step)
        part = total[span, :]
        for source, at, mixed in terms:
            part = part + dot_nn(source[at, span, :], mixed)
        row = lax.broadcasted_iota(jnp.int32, (step, wide), 0)
        col = lax.broadcasted_iota(jnp.int32, (step, wide), 1)
        chosen = jnp.where(lax.rem(row, nb) == lax.div(col, blk), part, 0.0).astype(BF16)
        masked[span, :] = chosen
        sums = sums + dot_tn(chosen, basis[span, :])
    new = sums[:blk]
    for b in range(1, nb):
        new = new + sums[b * blk : (b + 1) * blk]
    new_out[:blk, :], new_out[blk:, :] = split(new)


def join_kernel(kept, got_b, got_a, got_ab, new, out):
    n = kept.shape[0]
    total = kept[...] + value(got_b, 0, n) + (value(got_a, 0, n) + value(got_ab, 0, n))
    out[:n, :], out[n : 2 * n, :] = split(total)
    out[2 * n :, :] = new[...]


def turn_kernel(nb, images, masked, rotation, far, held, sems):
    old = images.shape[1]
    tail = rotation[old:, :]
    deep = jnp.concatenate([tail] * nb, axis=0)
    put(
        far,
        held,
        sems,
        PIECES,
        lambda span: (dot_nn(images[span, :], rotation[:old, :]) + dot_nn(masked[span, :], deep)).astype(BF16),
    )


def value(ref, start, count):
    return ref[start : start + count, :].astype(F32) + ref[start + count : start + 2 * count, :].astype(F32)


def extra_kernel(n, blk, pay, got, out):
    out[:n, :], out[n : 2 * n, :] = split(value(pay, 0, n) + value(got, 0, n))
    out[2 * n : 2 * n + blk, :], out[2 * n + blk :, :] = split(value(pay, 2 * n, blk) + value(got, 2 * n, blk))


def settle_kernel(n, blk, scale, pay, got, out):
    out[:n, :] = ((value(pay, 0, n) + value(got, 0, n)) * scale).astype(BF16)
    out[n : n + blk, :], out[n + blk :, :] = split(value(pay, 2 * n, blk) + value(got, 2 * n, blk))


def grow_kernel(n, blk, chooser, pay, got, out):
    bit = chooser(*place())
    out[rows_at(bit, n), :] = pay[:n, :]
    out[rows_at(1 - bit, n), :] = got[:n, :]
    out[2 * n : 2 * n + blk, :], out[2 * n + blk :, :] = split(value(pay, n, blk) + value(got, n, blk))


def join_four_kernel(n, blk, first, second, pay, got_a, got_b, got_ab, out):
    spot = place()
    a, b = first(*spot), second(*spot)
    out[rows_at(2 * b + a, n), :] = pay[:n, :]
    out[rows_at(2 * b + 1 - a, n), :] = got_a[:n, :]
    out[rows_at(2 * (1 - b) + a, n), :] = got_b[:n, :]
    out[rows_at(2 * (1 - b) + 1 - a, n), :] = got_ab[:n, :]
    new = (value(pay, n, blk) + value(got_a, n, blk)) + (value(got_b, n, blk) + value(got_ab, n, blk))
    out[4 * n : 4 * n + blk, :], out[4 * n + blk :, :] = split(new)


def early_kernel(n, pay, far, held, sem):
    core = place()[0]
    width = held.shape[1]
    held[...] = pay[:n, :width].astype(F32)
    copy = pltpu.make_async_copy(held, far.at[rows_at(core, n), :width], sem)
    copy.start()
    copy.wait()


def final_kernel(n, blk, scale, pay, got, begun, far, held, edge, sems):
    nvec = far.shape[1]
    core = place()[0]
    width = nvec - LANES
    new = (value(pay, n, blk) + value(got, n, blk)) * scale
    tall = jnp.concatenate([jnp.zeros((LANES - blk, nvec), F32), new], axis=0)
    step = n // 2
    copies = []
    for i in range(2):
        held[i * step : (i + 1) * step, :width] = got[i * step : (i + 1) * step, :width].astype(F32)
        span = pl.ds(pl.multiple_of((1 - core) * n + i * step, step), step)
        copies.append(pltpu.make_async_copy(held.at[pl.ds(i * step, step)], far.at[span, :width], sems.at[i]))
        copies[-1].start()
    lane = lax.broadcasted_iota(jnp.int32, (n, LANES), 1)
    edge[...] = tall.T
    for source, side in ((pay, core), (got, 1 - core)):
        span = rows_at(side, n)
        edge[span, :] = jnp.where(lane < LANES - blk, source[:n, width:].astype(F32), edge[span, :])
    copies.append(pltpu.make_async_copy(edge, far.at[:, width:], sems.at[2]))
    copies[-1].start()
    for copy in copies:
        copy.wait()


def program(basis, images, hops, neighbours, rotation):
    nb, modes_here, nvec = basis.shape
    old = images.shape[2]
    blk = nvec - old
    sites = lax.axis_size("site")
    spots = lax.axis_size("mode")
    count = sites * spots
    rows = nb * modes_here
    coarse = hops.shape[3]
    wide = nb * blk
    chunk = wide * LANES // nvec
    scale = 1.0 / math.sqrt(count * rows)

    def send(x, first, second):
        pairs = [(d, d ^ hop) for d in range(count) for hop in [second if d % 2 else first] if hop]
        return lax.ppermute(x, BOTH, pairs)

    core_hop, x_hop, y_hop, z0_hop, z1_hop = 1, 2, spots, 2 * spots, 4 * spots

    flat_basis = jnp.transpose(basis, (1, 0, 2)).reshape(rows, nvec)
    flat_images = jnp.transpose(images, (1, 0, 2)).reshape(rows, old)
    flat_hops = jnp.transpose(hops, (1, 2, 0, 3)).reshape(hops.shape[1], rows, coarse)
    half = nvec // 2
    n = half // 8
    near_order = [0] if sites > 8 else [0, 7, 8]
    far_order = [hop for hop in range(hops.shape[1]) if hop not in near_order]
    pay0, basis_here, images_here, shift, perms = call(
        functools.partial(open_kernel, nb, spots, near_order),
        (
            shaped(nvec + chunk, nvec, BF16),
            shaped(rows, nvec, BF16),
            shaped(rows, old, BF16),
            shaped(coarse // 2, spots * LANES // 2, BF16),
            jax.ShapeDtypeStruct((hops.shape[1], 2 * wide, wide), BF16),
        ),
        stay(flat_basis),
        stay(flat_images),
        stay(neighbours),
        far=(0, 1, 2),
        scratch=[
            pltpu.VMEM(neighbours.shape, jnp.int32),
            pltpu.SemaphoreType.DMA((2 * PIECES + 1,)),
        ],
    )

    def fetched(order):
        return call(
            functools.partial(fetch_kernel, order),
            jax.ShapeDtypeStruct((len(order), rows, coarse), BF16),
            stay(flat_hops),
            far=(0,),
            scratch=[pltpu.SemaphoreType.DMA((len(order),))],
        )

    got0 = send(pay0, core_hop, core_hop)
    groups = (near_order[:2], [2, 5, 3, 6] + near_order[2:], near_order[2:], [hop for hop in far_order if hop in (1, 4, 7, 8)])
    near_hops = fetched(groups[0])
    kept0 = call(keep_kernel, shaped(half, nvec, F32), basis_here, images_here)
    more_hops = fetched(groups[1])
    pay1, kept1, pair = call(
        second_kernel,
        (shaped(half + 2 * chunk, nvec, BF16), shaped(half // 2, nvec, F32), shaped(2 * chunk, nvec, BF16)),
        kept0,
        got0,
        pay0,
    )
    got1 = send(pay1, x_hop, y_hop)
    far = send(pair, 0, z1_hop)
    pay2, pay_a, pay_ab, kept2 = call(
        third_kernel,
        (
            shaped(2 * n + 4 * chunk, nvec, BF16),
            shaped(2 * n, nvec, BF16),
            shaped(2 * n, nvec, BF16),
            shaped(n, nvec, F32),
        ),
        kept1,
        got1,
        pair,
        far,
    )
    got2 = send(pay2, z0_hop, x_hop)
    crossed = send(got1[half:, :], core_hop, core_hop)
    total, own = call(
        functools.partial(near_kernel, groups[0], groups[2]),
        (
            shaped(rows, wide, F32),
            shaped(coarse, wide, BF16),
        ),
        pair,
        got1,
        crossed,
        near_hops,
        more_hops,
        perms,
        shift,
    )
    times = []
    if sites > 8:
        gap = 8 * spots
        times = [lax.ppermute(own, BOTH, [((d + sign * gap) % count, d) for d in range(count)]) for sign in (1, -1)]
    got_a = send(pay_a, y_hop, z1_hop)
    got_ab = send(pay_ab, y_hop + z0_hop, z1_hop + x_hop)
    cross_pay = call(fourth_kernel, shaped(6 * chunk, nvec, BF16), got2, far)
    cross = send(cross_pay, core_hop, core_hop)
    total, next_hops = call(
        functools.partial(middle_kernel, groups[3]),
        (shaped(rows, wide, F32), jax.ShapeDtypeStruct((len(groups[3]), rows, coarse), BF16)),
        own,
        got2,
        got1,
        total,
        more_hops,
        stay(flat_hops),
        perms,
        shift,
        far=(5,),
        scratch=[pltpu.SemaphoreType.DMA((len(groups[3]),))],
    )
    masked, new = call(
        functools.partial(far_kernel, nb, blk, groups[3]),
        (shaped(rows, wide, BF16), shaped(2 * blk, nvec, BF16)),
        own,
        got2,
        cross,
        far,
        crossed,
        total,
        basis_here,
        next_hops,
        more_hops,
        perms,
        shift,
        *times,
    )
    payc = call(join_kernel, shaped(2 * n + 2 * blk, nvec, BF16), kept2, got2, got_a, got_ab, new)
    turned = [pltpu.VMEM((rows, nvec), BF16), pltpu.SemaphoreType.DMA((PIECES,))]
    gotc = send(payc, z1_hop, z0_hop)
    turned_images = call(
        functools.partial(turn_kernel, nb),
        shaped(rows, nvec, BF16),
        images_here,
        masked,
        rotation,
        out_far=True,
        scratch=turned,
    )
    hop = 8 * spots
    while hop < count:
        payc = call(functools.partial(extra_kernel, n, blk), shaped(2 * n + 2 * blk, nvec, BF16), payc, gotc)
        gotc = send(payc, hop, hop)
        hop *= 2
    payc = call(functools.partial(settle_kernel, n, blk, scale), shaped(n + 2 * blk, nvec, BF16), payc, gotc)
    turned_basis = call(
        rotate_kernel, shaped(rows, nvec, BF16), basis_here, rotation, out_far=True, scratch=turned
    )
    gotc = send(payc, y_hop, z1_hop)
    payc = call(
        functools.partial(grow_kernel, n, blk, lambda core, half, y, z0, z1: pick(core, y, z1)),
        shaped(2 * n + 2 * blk, nvec, BF16),
        payc,
        gotc,
    )
    n *= 2
    got_ab = send(payc, z0_hop + x_hop, x_hop + y_hop)
    got_b = send(payc, x_hop, y_hop)
    got_a = send(payc, z0_hop, x_hop)
    payc = call(
        functools.partial(
            join_four_kernel,
            n,
            blk,
            lambda core, half, y, z0, z1: pick(core, z0, half),
            lambda core, half, y, z0, z1: pick(core, half, y),
        ),
        shaped(4 * n + 2 * blk, nvec, BF16),
        payc,
        got_a,
        got_b,
        got_ab,
    )
    n *= 4
    gotc = send(payc, core_hop, core_hop)
    begun = call(
        functools.partial(early_kernel, n),
        shaped(nvec, nvec, F32),
        payc,
        out_far=True,
        scratch=[pltpu.VMEM((n, nvec - LANES), F32), pltpu.SemaphoreType.DMA],
    )
    projected = call(
        functools.partial(final_kernel, n, blk, scale),
        shaped(nvec, nvec, F32),
        payc,
        gotc,
        begun,
        far=(2,),
        out_far=True,
        alias={2: 0},
        scratch=[
            pltpu.VMEM((n, nvec - LANES), F32),
            pltpu.VMEM((nvec, LANES), F32),
            pltpu.SemaphoreType.DMA((3,)),
        ],
    )

    def back(x):
        return jnp.transpose(x.reshape(modes_here, nb, nvec), (1, 0, 2))

    return projected, back(turned_basis), back(turned_images)


def solution(mesh):
    placed = (
        P("site", "mode", None),
        P("site", "mode", None),
        P("site", None, "mode", None),
        P("site", None),
        P(),
    )
    return jax.shard_map(
        program,
        mesh=mesh,
        in_specs=placed,
        out_specs=(P(), P("site", "mode", None), P("site", "mode", None)),
        check_vma=False,
    )
```

```python
import functools
import math

import jax
import jax.numpy as jnp
from jax import lax
from jax.experimental import pallas as pl
from jax.experimental.pallas import tpu as pltpu
from jax.sharding import PartitionSpec as P


F32 = jnp.float32
BF16 = jnp.bfloat16
BOTH = ("site", "mode")
LANES = 128
PIECES = 2


def dot_nn(a, b):
    return lax.dot_general(a, b, (((1,), (0,)), ((), ())), preferred_element_type=F32)


def dot_tn(a, b):
    return lax.dot_general(a, b, (((0,), (0,)), ((), ())), preferred_element_type=F32)


def onehot(shape, test):
    rows = lax.broadcasted_iota(jnp.int32, shape, 0)
    cols = lax.broadcasted_iota(jnp.int32, shape, 1)
    return jnp.where(test(rows, cols), 1.0, 0.0).astype(BF16)


def split(x):
    high = x.astype(BF16)
    low = (x - high.astype(F32)).astype(BF16)
    return high, low


def place():
    mode = lax.axis_index("mode")
    site = lax.axis_index("site")
    core = lax.rem(mode, 2)
    half = lax.div(mode, 2)
    y = lax.rem(site, 2)
    z0 = lax.rem(lax.div(site, 2), 2)
    z1 = lax.rem(lax.div(site, 4), 2)
    return core, half, y, z0, z1


def pick(core, first, second):
    return first * (1 - core) + second * core


def rows_at(index, count):
    return pl.ds(pl.multiple_of(index * count, count), count)


def call(kernel, outs, *args, scratch=(), flops=10**8, moved=2 * 10**6, smem=(), far=(), out_far=False, alias={}):
    vmem = pl.BlockSpec(memory_space=pltpu.VMEM)
    scalars = pl.BlockSpec(memory_space=pltpu.SMEM)
    distant = pl.BlockSpec(memory_space=pltpu.HBM)
    return pl.pallas_call(
        kernel,
        out_shape=outs,
        in_specs=[scalars if i in smem else distant if i in far else vmem for i in range(len(args))],
        out_specs=jax.tree.map(lambda _: pl.BlockSpec(memory_space=pl.ANY) if out_far else vmem, outs),
        scratch_shapes=scratch,
        input_output_aliases=alias,
        compiler_params=pltpu.CompilerParams(vmem_limit_bytes=16 * 2**20),
        cost_estimate=pl.CostEstimate(flops=flops, bytes_accessed=moved, transcendentals=0),
    )(*args)


def stay(x):
    return pltpu.with_memory_space_constraint(x, pltpu.HBM)


def shaped(rows, cols, dtype):
    return jax.ShapeDtypeStruct((rows, cols), dtype)


def open_kernel(nb, spots, near, basis_far, images_far, table_far, pay, basis, images, shift, perms, table, sems):
    rows, nvec = basis.shape
    old = images.shape[1]
    blk = nvec - old
    step = rows // PIECES
    copies = []
    for j, (far, here) in enumerate(((basis_far, basis), (images_far, images))):
        for i in range(PIECES):
            span = pl.ds(i * step, step)
            copies.append(pltpu.make_async_copy(far.at[span], here.at[span], sems.at[j * PIECES + i]))
    small = pltpu.make_async_copy(table_far, table, sems.at[2 * PIECES])
    small.start()
    for copy in copies:
        copy.start()
    core = place()[0]
    top = nvec // 2
    wide = nb * blk
    share = 2 * shift.shape[0] // spots
    shift[...] = onehot(
        shift.shape,
        lambda r, c: (lax.rem(c, LANES) < share) & (lax.div(c, LANES) * share + lax.rem(c, LANES) == r),
    )
    gather = onehot((LANES, rows), lambda r, c: lax.div(c, nb) == r)
    spread = onehot((LANES, wide), lambda r, c: r - (LANES - blk) == lax.rem(c, blk))
    small.wait()
    choose(near, nb, blk, table[...], perms)
    for copy in copies[:PIECES]:
        copy.wait()
    tiled = dot_nn(basis[:, nvec - LANES :], spread)
    row = lax.broadcasted_iota(jnp.int32, (rows, wide), 0)
    col = lax.broadcasted_iota(jnp.int32, (rows, wide), 1)
    tiled = jnp.where(lax.rem(row, nb) == lax.div(col, blk), tiled, 0.0).astype(BF16)
    merged = dot_nn(gather, tiled).astype(BF16)
    groups = nvec // LANES
    each = LANES // groups
    for g in range(groups):
        pay[2 * top :, g * LANES : (g + 1) * LANES] = merged[g * each : (g + 1) * each]
    give = pl.ds(pl.multiple_of((1 - core) * top, top), top)
    part = None
    for i in range(PIECES):
        span = pl.ds(i * step, step)
        copies[PIECES + i].wait()
        piece = dot_tn(basis[span, give], images[span, :])
        part = piece if part is None else part + piece
    high, low = split(part)
    pay[:top, :old] = high
    pay[:top, old:] = jnp.zeros((top, blk), BF16)
    pay[top : 2 * top, :old] = low
    pay[top : 2 * top, old:] = jnp.zeros((top, blk), BF16)


def fetch_kernel(order, far, near, sems):
    copies = [pltpu.make_async_copy(far.at[hop], near.at[i], sems.at[i]) for i, hop in enumerate(order)]
    for copy in copies:
        copy.start()
    for copy in copies:
        copy.wait()


def keep_kernel(basis, images, kept):
    nvec = basis.shape[1]
    old = images.shape[1]
    core = place()[0]
    top = nvec // 2
    mine = basis[:, pl.ds(pl.multiple_of(core * top, top), top)]
    kept[:, :old] = dot_tn(mine, images[...])
    kept[:, old:] = jnp.zeros((top, nvec - old), F32)


def put(far, held, sems, pieces, work):
    step = held.shape[0] // pieces
    copies = []
    for i in range(pieces):
        span = pl.ds(i * step, step)
        held[span, :] = work(span)
        copy = pltpu.make_async_copy(held.at[span], far.at[span], sems.at[i])
        copy.start()
        copies.append(copy)
    for copy in copies:
        copy.wait()


def rotate_kernel(basis, rotation, far, held, sems):
    put(far, held, sems, PIECES, lambda span: dot_nn(basis[span, :], rotation[...]).astype(BF16))


def joined(kept, got, start, count):
    whole = kept.shape[0]
    rows = pl.ds(pl.multiple_of(start, count), count)
    lows = pl.ds(pl.multiple_of(start + whole, count), count)
    return kept[rows, :] + (got[rows, :].astype(F32) + got[lows, :].astype(F32))


def second_kernel(kept, got, pay, out, rest, pair):
    core, half, y, _, _ = place()
    whole = kept.shape[0]
    n = whole // 2
    bit = pick(core, half, y)
    out[:n, :], out[n : 2 * n, :] = split(joined(kept, got, (1 - bit) * n, n))
    rest[...] = joined(kept, got, bit * n, n)
    each = got.shape[0] - 2 * whole
    pair[rows_at(core, each), :] = pay[2 * whole :, :]
    pair[rows_at(1 - core, each), :] = got[2 * whole :, :]
    out[2 * n :, :] = pair[...]


def third_kernel(kept, got, pair, far, out, side_out, both_out, rest):
    core, half, y, z0, z1 = place()
    whole = kept.shape[0]
    n = whole // 4
    b, a = pick(core, z0, half), pick(core, y, z1)
    for target, spot in ((out, 2 * (1 - b) + a), (side_out, 2 * b + 1 - a), (both_out, 2 * (1 - b) + 1 - a)):
        target[:n, :], target[n : 2 * n, :] = split(joined(kept, got, spot * n, n))
    rest[...] = joined(kept, got, (2 * b + a) * n, n)
    each = pair.shape[0]
    at = pick(core, 1 - half, 0)
    out[pl.ds(pl.multiple_of(2 * n + at * each, each), each), :] = got[2 * whole :, :]
    out[pl.ds(pl.multiple_of(2 * n + (1 - at) * each, each), each), :] = jnp.where(
        core == 0, pair[...], far[...]
    )


def fourth_kernel(got, far, cross):
    area = cross.shape[0] - far.shape[0]
    cross[:area, :] = got[got.shape[0] - area :, :]
    cross[area:, :] = far[...]


def choose(near, nb, blk, table, perms):
    hops = perms.shape[0]
    wide = nb * blk
    row = lax.broadcasted_iota(jnp.int32, (2 * wide, wide), 0)
    col = lax.broadcasted_iota(jnp.int32, (hops - 1, wide), 1)
    repeat = onehot((nb, wide), lambda r, c: lax.div(c, blk) == r)
    entry = dot_tn(table.astype(F32).astype(BF16), repeat).astype(jnp.int32)
    piece = lax.div(entry, nb)
    wanted = (entry - piece * nb) * blk + lax.rem(col, blk)
    aside = wanted + jnp.where(piece > 0, wide, 0)
    perms[0] = onehot((2 * wide, wide), lambda r, c: r == c)
    for hop in range(1, hops):
        target = (wanted if hop in near else aside)[hop - 1 : hop, :]
        perms[hop] = jnp.where(row == target, 1.0, 0.0).astype(BF16)


def half_site(shift, piece):
    rows, nvec = piece.shape
    groups = nvec // LANES
    each = LANES // groups
    chunks = rows // each
    parts = [
        piece[m * each : (m + 1) * each, g * LANES : (g + 1) * LANES] for m in range(chunks) for g in range(groups)
    ]
    return dot_nn(shift, jnp.concatenate(parts, axis=0))


def ordered(half, first, second):
    low = jnp.where(half == 0, first, second)
    high = jnp.where(half == 0, second, first)
    return jnp.concatenate([low, high], axis=0).astype(BF16)


def pulled(order, far, near, sems):
    copies = [pltpu.make_async_copy(far.at[hop], near.at[i], sems.at[i]) for i, hop in enumerate(order)]
    for copy in copies:
        copy.start()
    return copies


def near_kernel(here, pair, got, crossed, hops, perms, shift, total, own_out):
    core, half, _, _, _ = place()
    each = pair.shape[0]
    wide = own_out.shape[1]
    area = got.shape[0]
    apart = jnp.where(core == 0, got[area - each :, :], crossed[...])
    own = ordered(half, half_site(shift[...], pair[...]), half_site(shift[...], apart))
    own_out[...] = own
    rows = total.shape[0]
    terms = [(hops, i, hop) for i, hop in enumerate(here)]
    mixed = [dot_nn(own, perms[hop, :wide, :]).astype(BF16) for _, _, hop in terms]
    step = rows // 2
    for r in range(2):
        span = pl.ds(r * step, step)
        part = None
        for (source, at, _), term in zip(terms, mixed):
            piece = dot_nn(source[at, span, :], term)
            part = piece if part is None else part + piece
        total[span, :] = part


def mixture(perms, own, site, hop):
    return dot_nn(jnp.concatenate([own[...], site], axis=1), perms[hop]).astype(BF16)


def middle_kernel(ahead, later, own, got2, got1, total, hops, hops_far, perms, shift, out, next_hops, sems):
    copies = pulled(ahead, hops_far, next_hops, sems)
    core, half, _, _, _ = place()
    first = core == 0
    each = 2 * LANES * LANES // got2.shape[1]
    mine = got2[got2.shape[0] - 2 * each :, :]
    move = shift[...]
    site = ordered(
        pick(core, 0, half),
        half_site(move, jnp.where(first, mine[:each], got1[got1.shape[0] - each :, :])),
        half_site(move, jnp.where(first, mine[each:], mine[:each])),
    )
    mixed = [mixture(perms, own, site, 2 + core + 3 * i) for i in range(2)]
    wide = own.shape[1]
    plain = [dot_nn(own[...], perms[hop, :wide, :]).astype(BF16) for hop in later]
    step = out.shape[0] // 2
    for r in range(2):
        span = pl.ds(r * step, step)
        part = total[span, :]
        for i in range(2):
            part = part + dot_nn(hops[2 * core + i, span, :], mixed[i])
        for i, term in enumerate(plain):
            part = part + dot_nn(hops[4 + i, span, :], term)
        out[span, :] = part
    for copy in copies:
        copy.wait()


def far_kernel(nb, blk, order, own, got2, cross, far, crossed, total, basis, hops, more, perms, shift, *refs):
    times, (masked, new_out) = refs[:-2], refs[-2:]
    core, half, _, _, _ = place()
    each = far.shape[0]
    wide = own.shape[1]
    rows = basis.shape[0]
    nvec = basis.shape[1]
    first = core == 0
    mine = got2[got2.shape[0] - 2 * each :, :]
    theirs = cross[: 2 * each, :]
    move = shift[...]
    site = ordered(
        pick(core, half, 0),
        half_site(move, jnp.where(first, crossed[...], theirs[:each])),
        half_site(move, jnp.where(first, theirs[:each], theirs[each:])),
    )
    long_site = ordered(
        half,
        half_site(move, jnp.where(first, cross[2 * each :, :], far[...])),
        half_site(move, jnp.where(first, theirs[each:], mine[each:])),
    )
    terms = [(more, 2 * (1 - core) + i, mixture(perms, own, site, 3 - core + 3 * i)) for i in range(2)]
    for i, hop in enumerate(order):
        term = long_site if hop in (1, 4) else times[hop - 7][...]
        terms.append((hops, i, mixture(perms, own, term, hop)))
    step = rows // 2
    sums = jnp.zeros((wide, nvec), F32)
    for r in range(2):
        span = pl.ds(r * step, step)
        part = total[span, :]
        for source, at, mixed in terms:
            part = part + dot_nn(source[at, span, :], mixed)
        row = lax.broadcasted_iota(jnp.int32, (step, wide), 0)
        col = lax.broadcasted_iota(jnp.int32, (step, wide), 1)
        chosen = jnp.where(lax.rem(row, nb) == lax.div(col, blk), part, 0.0).astype(BF16)
        masked[span, :] = chosen
        sums = sums + dot_tn(chosen, basis[span, :])
    new = sums[:blk]
    for b in range(1, nb):
        new = new + sums[b * blk : (b + 1) * blk]
    new_out[:blk, :], new_out[blk:, :] = split(new)


def join_kernel(kept, got_b, got_a, got_ab, new, out):
    n = kept.shape[0]
    total = kept[...] + value(got_b, 0, n) + (value(got_a, 0, n) + value(got_ab, 0, n))
    out[:n, :], out[n : 2 * n, :] = split(total)
    out[2 * n :, :] = new[...]


def turn_kernel(nb, images, masked, rotation, far, held, sems):
    old = images.shape[1]
    tail = rotation[old:, :]
    deep = jnp.concatenate([tail] * nb, axis=0)
    put(
        far,
        held,
        sems,
        PIECES,
        lambda span: (dot_nn(images[span, :], rotation[:old, :]) + dot_nn(masked[span, :], deep)).astype(BF16),
    )


def value(ref, start, count):
    return ref[start : start + count, :].astype(F32) + ref[start + count : start + 2 * count, :].astype(F32)


def extra_kernel(n, blk, pay, got, out):
    out[:n, :], out[n : 2 * n, :] = split(value(pay, 0, n) + value(got, 0, n))
    out[2 * n : 2 * n + blk, :], out[2 * n + blk :, :] = split(value(pay, 2 * n, blk) + value(got, 2 * n, blk))


def settle_kernel(n, blk, scale, pay, got, out):
    out[:n, :] = ((value(pay, 0, n) + value(got, 0, n)) * scale).astype(BF16)
    out[n : n + blk, :], out[n + blk :, :] = split(value(pay, 2 * n, blk) + value(got, 2 * n, blk))


def grow_kernel(n, blk, chooser, pay, got, out):
    bit = chooser(*place())
    out[rows_at(bit, n), :] = pay[:n, :]
    out[rows_at(1 - bit, n), :] = got[:n, :]
    out[2 * n : 2 * n + blk, :], out[2 * n + blk :, :] = split(value(pay, n, blk) + value(got, n, blk))


def join_four_kernel(n, blk, first, second, pay, got_a, got_b, got_ab, out):
    spot = place()
    a, b = first(*spot), second(*spot)
    out[rows_at(2 * b + a, n), :] = pay[:n, :]
    out[rows_at(2 * b + 1 - a, n), :] = got_a[:n, :]
    out[rows_at(2 * (1 - b) + a, n), :] = got_b[:n, :]
    out[rows_at(2 * (1 - b) + 1 - a, n), :] = got_ab[:n, :]
    new = (value(pay, n, blk) + value(got_a, n, blk)) + (value(got_b, n, blk) + value(got_ab, n, blk))
    out[4 * n : 4 * n + blk, :], out[4 * n + blk :, :] = split(new)


def early_kernel(n, pay, far, held, sem):
    core = place()[0]
    width = held.shape[1]
    held[...] = pay[:n, :width].astype(F32)
    copy = pltpu.make_async_copy(held, far.at[rows_at(core, n), :width], sem)
    copy.start()
    copy.wait()


def final_kernel(n, blk, scale, pay, got, begun, far, held, edge, sems):
    nvec = far.shape[1]
    core = place()[0]
    width = nvec - LANES
    new = (value(pay, n, blk) + value(got, n, blk)) * scale
    tall = jnp.concatenate([jnp.zeros((LANES - blk, nvec), F32), new], axis=0)
    step = n // 2
    copies = []
    for i in range(2):
        held[i * step : (i + 1) * step, :width] = got[i * step : (i + 1) * step, :width].astype(F32)
        span = pl.ds(pl.multiple_of((1 - core) * n + i * step, step), step)
        copies.append(pltpu.make_async_copy(held.at[pl.ds(i * step, step)], far.at[span, :width], sems.at[i]))
        copies[-1].start()
    lane = lax.broadcasted_iota(jnp.int32, (n, LANES), 1)
    edge[...] = tall.T
    for source, side in ((pay, core), (got, 1 - core)):
        span = rows_at(side, n)
        edge[span, :] = jnp.where(lane < LANES - blk, source[:n, width:].astype(F32), edge[span, :])
    copies.append(pltpu.make_async_copy(edge, far.at[:, width:], sems.at[2]))
    copies[-1].start()
    for copy in copies:
        copy.wait()


def program(basis, images, hops, neighbours, rotation):
    nb, modes_here, nvec = basis.shape
    old = images.shape[2]
    blk = nvec - old
    sites = lax.axis_size("site")
    spots = lax.axis_size("mode")
    count = sites * spots
    rows = nb * modes_here
    coarse = hops.shape[3]
    wide = nb * blk
    chunk = wide * LANES // nvec
    scale = 1.0 / math.sqrt(count * rows)

    def send(x, first, second):
        pairs = [(d, d ^ hop) for d in range(count) for hop in [second if d % 2 else first] if hop]
        return lax.ppermute(x, BOTH, pairs)

    core_hop, x_hop, y_hop, z0_hop, z1_hop = 1, 2, spots, 2 * spots, 4 * spots

    flat_basis = jnp.transpose(basis, (1, 0, 2)).reshape(rows, nvec)
    flat_images = jnp.transpose(images, (1, 0, 2)).reshape(rows, old)
    flat_hops = jnp.transpose(hops, (1, 2, 0, 3)).reshape(hops.shape[1], rows, coarse)
    half = nvec // 2
    n = half // 8
    near_order = [0] if sites > 8 else [0, 7, 8]
    far_order = [hop for hop in range(hops.shape[1]) if hop not in near_order]
    pay0, basis_here, images_here, shift, perms = call(
        functools.partial(open_kernel, nb, spots, near_order),
        (
            shaped(nvec + chunk, nvec, BF16),
            shaped(rows, nvec, BF16),
            shaped(rows, old, BF16),
            shaped(coarse // 2, spots * LANES // 2, BF16),
            jax.ShapeDtypeStruct((hops.shape[1], 2 * wide, wide), BF16),
        ),
        stay(flat_basis),
        stay(flat_images),
        stay(neighbours),
        far=(0, 1, 2),
        scratch=[
            pltpu.VMEM(neighbours.shape, jnp.int32),
            pltpu.SemaphoreType.DMA((2 * PIECES + 1,)),
        ],
    )

    def fetched(order):
        return call(
            functools.partial(fetch_kernel, order),
            jax.ShapeDtypeStruct((len(order), rows, coarse), BF16),
            stay(flat_hops),
            far=(0,),
            scratch=[pltpu.SemaphoreType.DMA((len(order),))],
        )

    got0 = send(pay0, core_hop, core_hop)
    groups = (near_order[:2], [2, 5, 3, 6] + near_order[2:], near_order[2:], [hop for hop in far_order if hop in (1, 4, 7, 8)])
    near_hops = fetched(groups[0])
    kept0 = call(keep_kernel, shaped(half, nvec, F32), basis_here, images_here)
    more_hops = fetched(groups[1])
    pay1, kept1, pair = call(
        second_kernel,
        (shaped(half + 2 * chunk, nvec, BF16), shaped(half // 2, nvec, F32), shaped(2 * chunk, nvec, BF16)),
        kept0,
        got0,
        pay0,
    )
    got1 = send(pay1, x_hop, y_hop)
    far = send(pair, 0, z1_hop)
    pay2, pay_a, pay_ab, kept2 = call(
        third_kernel,
        (
            shaped(2 * n + 4 * chunk, nvec, BF16),
            shaped(2 * n, nvec, BF16),
            shaped(2 * n, nvec, BF16),
            shaped(n, nvec, F32),
        ),
        kept1,
        got1,
        pair,
        far,
    )
    got2 = send(pay2, z0_hop, x_hop)
    crossed = send(got1[half:, :], core_hop, core_hop)
    total, own = call(
        functools.partial(near_kernel, groups[0]),
        (
            shaped(rows, wide, F32),
            shaped(coarse, wide, BF16),
        ),
        pair,
        got1,
        crossed,
        near_hops,
        perms,
        shift,
    )
    times = []
    if sites > 8:
        gap = 8 * spots
        times = [lax.ppermute(own, BOTH, [((d + sign * gap) % count, d) for d in range(count)]) for sign in (1, -1)]
    got_a = send(pay_a, y_hop, z1_hop)
    got_ab = send(pay_ab, y_hop + z0_hop, z1_hop + x_hop)
    cross_pay = call(fourth_kernel, shaped(6 * chunk, nvec, BF16), got2, far)
    cross = send(cross_pay, core_hop, core_hop)
    total, next_hops = call(
        functools.partial(middle_kernel, groups[3], groups[2]),
        (shaped(rows, wide, F32), jax.ShapeDtypeStruct((len(groups[3]), rows, coarse), BF16)),
        own,
        got2,
        got1,
        total,
        more_hops,
        stay(flat_hops),
        perms,
        shift,
        far=(5,),
        scratch=[pltpu.SemaphoreType.DMA((len(groups[3]),))],
    )
    masked, new = call(
        functools.partial(far_kernel, nb, blk, groups[3]),
        (shaped(rows, wide, BF16), shaped(2 * blk, nvec, BF16)),
        own,
        got2,
        cross,
        far,
        crossed,
        total,
        basis_here,
        next_hops,
        more_hops,
        perms,
        shift,
        *times,
    )
    payc = call(join_kernel, shaped(2 * n + 2 * blk, nvec, BF16), kept2, got2, got_a, got_ab, new)
    turned = [pltpu.VMEM((rows, nvec), BF16), pltpu.SemaphoreType.DMA((PIECES,))]
    gotc = send(payc, z1_hop, z0_hop)
    turned_images = call(
        functools.partial(turn_kernel, nb),
        shaped(rows, nvec, BF16),
        images_here,
        masked,
        rotation,
        out_far=True,
        scratch=turned,
    )
    hop = 8 * spots
    while hop < count:
        payc = call(functools.partial(extra_kernel, n, blk), shaped(2 * n + 2 * blk, nvec, BF16), payc, gotc)
        gotc = send(payc, hop, hop)
        hop *= 2
    payc = call(functools.partial(settle_kernel, n, blk, scale), shaped(n + 2 * blk, nvec, BF16), payc, gotc)
    turned_basis = call(
        rotate_kernel, shaped(rows, nvec, BF16), basis_here, rotation, out_far=True, scratch=turned
    )
    gotc = send(payc, y_hop, z1_hop)
    payc = call(
        functools.partial(grow_kernel, n, blk, lambda core, half, y, z0, z1: pick(core, y, z1)),
        shaped(2 * n + 2 * blk, nvec, BF16),
        payc,
        gotc,
    )
    n *= 2
    got_ab = send(payc, z0_hop + x_hop, x_hop + y_hop)
    got_b = send(payc, x_hop, y_hop)
    got_a = send(payc, z0_hop, x_hop)
    payc = call(
        functools.partial(
            join_four_kernel,
            n,
            blk,
            lambda core, half, y, z0, z1: pick(core, z0, half),
            lambda core, half, y, z0, z1: pick(core, half, y),
        ),
        shaped(4 * n + 2 * blk, nvec, BF16),
        payc,
        got_a,
        got_b,
        got_ab,
    )
    n *= 4
    gotc = send(payc, core_hop, core_hop)
    begun = call(
        functools.partial(early_kernel, n),
        shaped(nvec, nvec, F32),
        payc,
        out_far=True,
        scratch=[pltpu.VMEM((n, nvec - LANES), F32), pltpu.SemaphoreType.DMA],
    )
    projected = call(
        functools.partial(final_kernel, n, blk, scale),
        shaped(nvec, nvec, F32),
        payc,
        gotc,
        begun,
        far=(2,),
        out_far=True,
        alias={2: 0},
        scratch=[
            pltpu.VMEM((n, nvec - LANES), F32),
            pltpu.VMEM((nvec, LANES), F32),
            pltpu.SemaphoreType.DMA((3,)),
        ],
    )

    def back(x):
        return jnp.transpose(x.reshape(modes_here, nb, nvec), (1, 0, 2))

    return projected, back(turned_basis), back(turned_images)


def solution(mesh):
    placed = (
        P("site", "mode", None),
        P("site", "mode", None),
        P("site", None, "mode", None),
        P("site", None),
        P(),
    )
    return jax.shard_map(
        program,
        mesh=mesh,
        in_specs=placed,
        out_specs=(P(), P("site", "mode", None), P("site", "mode", None)),
        check_vma=False,
    )
```
